32 devices in a mesh: outer: 4 (over y, x), inner: 8 (over z, core).
Axes of the slice: x: 2, y: 2, z: 4, core: 2. Of those that a mesh axis runs over, the one named last changes fastest.
Arguments:
- queries: bfloat16 [4096, 2048], P(('outer', 'inner')), may hold values from -6 to 6
- key_rows: bfloat16 [4096, 2048], P(('outer', 'inner')), may hold values from -6 to 6
- value_rows: bfloat16 [4096, 2048], P(('outer', 'inner')), may hold values from -6 to 6
- beta_logit: bfloat16 [4096, 16], P(('outer', 'inner')), may hold values from -8 to 2, as said below
- log_gate: bfloat16 [4096, 16], P(('outer', 'inner')), may hold values from -1 to 0, as said below
- out_grad: bfloat16 [4096, 2048], P(('outer', 'inner')), may hold values from -6 to 6
- block_states: float32 [4, 16, 128, 128], P('outer', 'inner'), may hold values from -4 to 4
Outputs:
- query_gradient: bfloat16 [4096, 2048], P(('outer', 'inner'))
- grad_keys: bfloat16 [4096, 2048], P(('outer', 'inner'))
- grad_values: bfloat16 [4096, 2048], P(('outer', 'inner'))
- grad_beta: bfloat16 [4096, 16], P(('outer', 'inner'))
- grad_gate: bfloat16 [4096, 16], P(('outer', 'inner'))
The draws below stay inside these ranges and needn't reach their ends.
Inputs may be any that keep to these rules, and one draw needn't show every extreme that they name: `beta_logit`: within each head the logits lie within 1 of a level drawn for each head. `log_gate`: negative in every entry.
All inputs are finite; a program needn't handle non-finite values.
Results may differ from the reference program's by a relative error of at most 0.002.
Values may be sent and summed in bfloat16 or wider, within the bound.
A program may use at most 128 MiB of HBM per device.

```python
import math
import jax
import jax.numpy as jnp
from jax import lax

H = 16
DK = 128
DV = 128
GROUP = 128
TOK_DEV = 128
TOKENS = 4096
N_OUTER = 4


def quick_heads(key):
    fast_share = 0.5
    return jax.random.bernoulli(jax.random.fold_in(key, 11), fast_share, (H,))


def draw_key_rows(key, part):
    sub_key = jax.random.fold_in(key, 53)
    shared = jax.random.normal(jax.random.fold_in(sub_key, 1), (H, DK), jnp.float32)
    amplitude = jax.random.uniform(jax.random.fold_in(sub_key, 2), (H,), jnp.float32, 0.8, 1.2)
    noise = jax.random.normal(jax.random.fold_in(sub_key, 3), (TOKENS, H, DK), jnp.float32)
    rows = noise + amplitude[None, :, None] * shared[None, :, :]
    return jnp.clip(rows, -6.0, 6.0).reshape(TOKENS, H * DK).astype(jnp.bfloat16)


def draw_beta_logit(key, part):
    sub_key = jax.random.fold_in(key, 23)
    centers = jax.random.uniform(jax.random.fold_in(sub_key, 1), (H,), jnp.float32, -6.5, -1.5)
    spread = jax.random.uniform(jax.random.fold_in(sub_key, 2), (TOKENS, H), jnp.float32, -1.0, 1.0)
    return (centers[None, :] + spread).astype(jnp.bfloat16)


def draw_log_gate(key, part):
    quick = quick_heads(key)
    sub_key = jax.random.fold_in(key, 37)
    quick_rate = jnp.exp(jax.random.uniform(jax.random.fold_in(sub_key, 1), (H,), jnp.float32, math.log(1.0 / 50.0), math.log(1.0 / 30.0)))
    slow_rate = jnp.exp(jax.random.uniform(jax.random.fold_in(sub_key, 2), (H,), jnp.float32, math.log(0.05), math.log(0.15))) / TOKENS
    decay_rate = jnp.where(quick, quick_rate, slow_rate)
    device_count = TOKENS // TOK_DEV
    device_factor = jnp.exp(jax.random.uniform(jax.random.fold_in(sub_key, 3), (device_count, H), jnp.float32, math.log(0.5), math.log(2.0)))
    owner = jnp.arange(TOKENS) // TOK_DEV
    per_token = device_factor[owner]
    rough = jax.random.uniform(jax.random.fold_in(sub_key, 4), (TOKENS, H), jnp.float32, 0.5, 1.5)
    initial_gate = -decay_rate[None, :] * per_token * rough
    spots = jax.random.randint(jax.random.fold_in(sub_key, 5), (2,), 0, TOKENS)
    total_quantity = jax.random.uniform(jax.random.fold_in(sub_key, 6), (2, H), jnp.float32, 0.22, 0.45)
    match_count = (jnp.arange(TOKENS)[:, None] == spots[None, :]).astype(jnp.float32)
    sudden_spikes = jnp.dot(match_count, total_quantity)
    return (initial_gate - sudden_spikes).astype(jnp.bfloat16)


def levels(stream_key, extent, cuts, smallest, top_value):
    level = 1.0
    for axis_at, blocks in cuts:
        draws = jax.random.uniform(jax.random.fold_in(jax.random.fold_in(stream_key, 6), axis_at), (blocks,), jnp.float32, smallest / len(cuts), top_value / len(cuts))
        level = level * jnp.repeat(jnp.exp(draws), extent[axis_at] // blocks).reshape((-1,) + (1,) * (len(extent) - 1 - axis_at))
    return level


def scatter_about(rng, extent, deviation, most, split=(), kind=jnp.bfloat16):
    values = jax.random.normal(rng, extent, jnp.float32) * deviation
    if len(split) > 0:
        values = levels(rng, extent, split, -0.22, 0.18) * values
    return jnp.clip(values, min=-most, max=most).astype(kind)


def setup_inputs(seed: int = 0) -> dict:
    streams_of = jax.random.split(jax.random.key(seed), 8)
    queries = scatter_about(streams_of[0], (TOKENS, H * DK), 1.0, 6.0, ((0, 32),))
    key_rows = draw_key_rows(jax.random.fold_in(streams_of[7], 71), 0)
    value_rows = scatter_about(streams_of[2], (TOKENS, H * DV), 1.0, 6.0, ((0, 32),))
    beta_logit = draw_beta_logit(jax.random.fold_in(streams_of[7], 71), 0)
    log_gate = draw_log_gate(jax.random.fold_in(streams_of[7], 71), 0)
    out_grad = scatter_about(streams_of[5], (TOKENS, H * DV), 1.0, 6.0, ((0, 32),))
    block_states = scatter_about(streams_of[6], (N_OUTER, H, DK, DV), 0.5, 4.0, ((0, 4), (1, 8)), jnp.float32)
    return {"queries": queries, "key_rows": key_rows, "value_rows": value_rows, "beta_logit": beta_logit, "log_gate": log_gate, "out_grad": out_grad, "block_states": block_states}


precise = lax.Precision.HIGHEST

def unit_rows(matrix):
    return matrix * lax.rsqrt(lax.optimization_barrier(jnp.sum(matrix * matrix, axis=-1, keepdims=True)) + 1e-06)

def group_step(carried, inputs):
    state_now, transition = carried
    query_part, key_part, value_part, strength, gate_part = inputs
    group_len = query_part.shape[1]
    key_width = key_part.shape[2]
    row_index = jnp.arange(group_len)[:, None]
    col_index = jnp.arange(group_len)[None, :]
    inclusive = row_index >= col_index
    strictly_lower = row_index > col_index
    cumulative = jnp.cumsum(gate_part, axis=1)
    gaps = cumulative[:, :, None] - cumulative[:, None, :]
    decay_mat = jnp.where(inclusive, jnp.exp(jnp.where(inclusive, gaps, 0.0)), 0.0)
    key_gram = jnp.einsum('hid,hjd->hij', key_part, key_part, precision=precise)
    lower_mat = strength[:, :, None] * jnp.where(strictly_lower, decay_mat, 0.0) * key_gram
    unit_lower = lower_mat + jnp.eye(group_len, dtype=jnp.float32)
    growth = jnp.exp(cumulative)
    right_side = jnp.concatenate([(strength * growth)[:, :, None] * key_part, strength[:, :, None] * value_part], axis=2)
    solution_matrix = lax.linalg.triangular_solve(unit_lower, right_side, left_side=True, lower=True, unit_diagonal=True)
    write_keys = solution_matrix[:, :, :key_width]
    write_values = solution_matrix[:, :, key_width:]
    new_values = write_values - jnp.einsum('hcd,hde->hce', write_keys, state_now, precision=precise)
    scores = jnp.einsum('hid,hjd->hij', query_part, key_part, precision=precise) * decay_mat
    output = jnp.einsum('hcd,hde->hce', query_part * growth[:, :, None], state_now, precision=precise)
    output = output + jnp.einsum('hij,hje->hie', scores, new_values, precision=precise)
    tail_decay = jnp.exp(cumulative[:, -1:] - cumulative)
    tail_keys = key_part * tail_decay[:, :, None]
    last_growth = growth[:, -1][:, None, None]
    state_next = last_growth * state_now + jnp.einsum('hcd,hce->hde', tail_keys, new_values, precision=precise)
    step_trans = last_growth * jnp.eye(key_width, dtype=jnp.float32) - jnp.einsum('hcd,hce->hde', tail_keys, write_keys, precision=precise)
    transition = jnp.einsum('hij,hjk->hik', step_trans, transition, precision=precise)
    return ((state_next, transition), output)

def block_forward(queries, keys_in, values, logits, gates, start_state, group_size):
    head_count, length, key_width = queries.shape
    group_count = length // group_size

    def to_groups(array_in):
        shaped = array_in.reshape((head_count, group_count, group_size) + array_in.shape[2:])
        return jnp.moveaxis(shaped, 1, 0)
    inputs = (to_groups(unit_rows(queries)), to_groups(unit_rows(keys_in)), to_groups(values), to_groups(jax.nn.sigmoid(logits)), to_groups(gates))
    identity = jnp.broadcast_to(jnp.eye(key_width, dtype=jnp.float32), (head_count, key_width, key_width))
    (final_state, transition), outputs = lax.scan(group_step, (start_state, identity), inputs)
    outputs = jnp.moveaxis(outputs, 0, 1).reshape(head_count, length, -1)
    return (outputs, final_state, transition)

def reference(queries, key_rows, value_rows, beta_logit, log_gate, out_grad, block_states):
    per_block = TOKENS // N_OUTER

    def arrange(array_in, width):
        return array_in.astype(jnp.float32).reshape(N_OUTER, per_block, H, width).transpose(0, 2, 1, 3)

    def arrange_small(array_in):
        return array_in.astype(jnp.float32).reshape(N_OUTER, per_block, H).transpose(0, 2, 1)
    inputs = (arrange(queries, DK), arrange(key_rows, DK), arrange(value_rows, DV), arrange_small(beta_logit), arrange_small(log_gate), arrange(out_grad, DV), block_states)

    def backward(incoming, pieces):
        query_in, key_in, value_in, logit_in, gate_in, cotangent, start_state = pieces

        def forward(query_arg, key_arg, value_arg, logit_arg, gate_arg, state_arg):
            outputs, final_state, unused = block_forward(query_arg, key_arg, value_arg, logit_arg, gate_arg, state_arg, GROUP)
            return (outputs, final_state)
        unused_out, pull_back = jax.vjp(forward, query_in, key_in, value_in, logit_in, gate_in, start_state)
        gradients = pull_back((cotangent, incoming))
        return (gradients[5], gradients[:5])
    unused_carry, gradients = lax.scan(backward, jnp.zeros((H, DK, DV), jnp.float32), inputs, reverse=True)

    def restore(array_in):
        return array_in.transpose(0, 2, 1, 3).reshape(TOKENS, -1).astype(jnp.bfloat16)

    def restore_small(array_in):
        return array_in.transpose(0, 2, 1).reshape(TOKENS, H).astype(jnp.bfloat16)
    return (restore(gradients[0]), restore(gradients[1]), restore(gradients[2]), restore_small(gradients[3]), restore_small(gradients[4]))
```

```python
import functools

import jax
import jax.numpy as jnp
from jax import lax
from jax.experimental import pallas as pl
from jax.experimental.pallas import tpu as pltpu
from jax.sharding import PartitionSpec as P

D = 128
C = 128
BF = jnp.bfloat16
F32 = jnp.float32
MESH = pl.DeviceIdType.MESH
VM = pl.BlockSpec(memory_space=pltpu.VMEM)
DIMS = {"nn": ((1,), (0,)), "nt": ((1,), (1,)), "tn": ((0,), (0,))}


def split(x):
    hi = x.astype(BF)
    return hi, (x - hi.astype(F32)).astype(BF)


def exact(x):
    return x.astype(BF), None


def dot(a, b, mode):
    return lax.dot_general(a, b, (DIMS[mode], ((), ())), preferred_element_type=F32)


def mm(a, b, mode):
    ka = 0 if mode == "tn" else 1
    kb = 1 if mode == "nt" else 0
    (ah, al), (bh, bl) = a, b
    if al is None and bl is None:
        return dot(ah, bh, mode)
    if al is None:
        return dot(jnp.concatenate([ah, ah], ka), jnp.concatenate([bh, bl], kb), mode)
    left = jnp.concatenate([ah, al], ka)
    if bl is None:
        return dot(left, jnp.concatenate([bh, bh], kb), mode)
    top = jnp.concatenate([bh, bl], 1 - kb)
    low = jnp.concatenate([bh, jnp.zeros_like(bl)], 1 - kb)
    both = dot(left, jnp.concatenate([top, low], kb), mode)
    n = both.shape[1] // 2
    return both[:, :n] + both[:, n:]


def iotas():
    return lax.broadcasted_iota(jnp.int32, (C, C), 0), lax.broadcasted_iota(jnp.int32, (C, C), 1)


def ones_where(mask):
    return jnp.where(mask, 1.0, 0.0).astype(BF)


def unit(x):
    r = lax.rsqrt(jnp.sum(x * x, axis=1, keepdims=True) + 1e-06)
    return x * r, r


def decays(gate, row, col):
    wide = gate
    rhs = jnp.concatenate([wide, jnp.where(row > col, wide, 0.0)], 1).astype(BF)
    both = dot(ones_where(row >= col), rhs, "nn")
    after = dot(ones_where(row < col), wide.astype(BF), "nn")
    pair = jnp.where(row >= col, jnp.exp(both[:, C:]), 0.0)
    return jnp.exp(both[:, :C]), jnp.exp(after), pair


def inverses(lowers, row, col):
    eye = jnp.where(row == col, 1.0, 0.0)
    done = [eye - jnp.where((row // 2 == col // 2), low, 0.0) for low in lowers]
    size = 2
    while size < C:
        pick = (row // (2 * size) == col // (2 * size)) & (row // size != col // size)
        halves = [split(t) for t in done]
        mids = [mm(t, split(jnp.where(pick, low, 0.0)), "nn") for t, low in zip(halves, lowers)]
        done = [t - mm(split(m), h, "nn") for t, m, h in zip(done, mids, halves)]
        size *= 2
    return done


def head_columns(b_ref, g_ref, h):
    heads = b_ref.shape[0]
    pick = ones_where(lax.broadcasted_iota(jnp.int32, (heads, C), 0) == h)
    return jax.nn.sigmoid(dot(b_ref[...], pick, "tn")), dot(g_ref[...], pick, "tn")


def grams(qn, kn, pair, row, col):
    qs, ks = split(qn), split(kn)
    left = (jnp.concatenate([qs[0], ks[0]], 0), jnp.concatenate([qs[1], ks[1]], 0))
    both = mm(left, ks, "nt")
    return both[:C] * pair, jnp.where(row > col, both[C:] * pair, 0.0)


def columns(h):
    return pl.ds(pl.multiple_of(h * D, D), D)


def group_start(hs, args, keep):
    b_ref, g_ref, q_ref, k_ref, _, c_ref = args
    row, col = iotas()
    cols = [head_columns(b_ref, g_ref, h) for h in hs]
    qns = [unit(q_ref[:, columns(h)].astype(F32))[0] for h in hs]
    kns = [unit(k_ref[:, columns(h)].astype(F32))[0] for h in hs]
    decs = [decays(gate, row, col) for _, gate in cols]
    gms = [grams(qn, kn, pair, row, col) for qn, kn, (_, _, pair) in zip(qns, kns, decs)]
    cots = [exact(c_ref[:, columns(h)]) for h in hs]
    qparts = [mm(cot, split(qn * d[0]), "tn") for cot, qn, d in zip(cots, qns, decs)]
    pcs = [mm(split(scores), cot, "tn") for (scores, _), cot in zip(gms, cots)]
    for j, h in enumerate(hs):
        for name, value in (
            ("beta", cols[j][0]), ("growth", decs[j][0]), ("tail", decs[j][1]),
            ("pair", decs[j][2]), ("scores", gms[j][0]), ("gram", gms[j][1]),
            ("pc", pcs[j]), ("x", qparts[j]),
        ):
            keep[name][h] = value


def group_solve(hs, keep):
    row, col = iotas()
    lowers = [keep["beta"][h] * keep["gram"][h] for h in hs]
    for h, inv in zip(hs, inverses(lowers, row, col)):
        keep["inv"][h] = inv


def group_end(hs, args, keep, pack):
    _, _, _, k_ref, v_ref, _ = args
    row, col = iotas()
    eye = row == col
    kns = [unit(k_ref[:, columns(h)].astype(F32))[0] for h in hs]
    betas = [keep["beta"][h] for h in hs]
    grows = [keep["growth"][h] for h in hs]
    invs = [split(keep["inv"][h]) for h in hs]
    wks = [mm(i, split(b * g * kn), "nn") for i, b, g, kn in zip(invs, betas, grows, kns)]
    wvs = [
        mm(i, split(b * v_ref[:, columns(h)].astype(F32)), "nn")
        for i, b, h in zip(invs, betas, hs)
    ]
    tss = [split(kn * keep["tail"][h]) for kn, h in zip(kns, hs)]
    wss = [split(wk) for wk in wks]
    lasts = [jnp.where(eye, jnp.broadcast_to(g[C - 1 :, :], (C, C)), 0.0) for g in grows]
    ms = [last - mm(ts, ws, "tn") for last, ts, ws in zip(lasts, tss, wss)]
    rs = [keep["x"][h] - mm(split(keep["pc"][h]), ws, "tn") for h, ws in zip(hs, wss)]
    ads = [mm(ts, split(wv), "tn") for ts, wv in zip(tss, wvs)]
    for j, h in enumerate(hs):
        keep["wk"][h] = wks[j]
        keep["wv"][h] = wvs[j]
        pack[0, h, 0] = ms[j]
        pack[0, h, 1] = ads[j]
        pack[0, h, 2] = rs[j]


def state_stage(hs, args, keep, dq_ref):
    _, _, q_ref, k_ref, _, c_ref = args
    qus = [unit(q_ref[:, columns(h)].astype(F32)) for h in hs]
    kns = [unit(k_ref[:, columns(h)].astype(F32))[0] for h in hs]
    cots = [exact(c_ref[:, columns(h)]) for h in hs]
    sss = [split(keep["st"][h]) for h in hs]
    news = [keep["wv"][h] - mm(split(keep["wk"][h]), ss, "nn") for h, ss in zip(hs, sss)]
    dqgs = [keep["growth"][h] * mm(cot, ss, "nt") for h, cot, ss in zip(hs, cots, sss)]
    dscs = [mm(cot, split(new), "nt") for cot, new in zip(cots, news)]
    b1s = [split(dsc * keep["pair"][h]) for h, dsc in zip(hs, dscs)]
    dqns = [mm(b1, split(kn), "nn") + dqg for b1, kn, dqg in zip(b1s, kns, dqgs)]
    wks = [mm(b1, split(qn), "tn") for b1, (qn, _) in zip(b1s, qus)]
    dqs = [
        (qr * (dqn - qn * jnp.sum(dqn * qn, axis=1, keepdims=True))).astype(BF)
        for (qn, qr), dqn in zip(qus, dqns)
    ]
    zs = [dsc * keep["scores"][h] for h, dsc in zip(hs, dscs)]
    for j, h in enumerate(hs):
        dq_ref[:, columns(h)] = dqs[j]
        keep["wv"][h] = news[j]
        keep["wk"][h] = wks[j]
        keep["z"][h] = zs[j]
        keep["x"][h] = dqgs[j] * qus[j][0]


def grad_stage(hs, args, keep, dk_ref, dv_ref, db_acc, dg_acc):
    _, _, _, k_ref, v_ref, _ = args
    row, col = iotas()
    upper = ones_where(row <= col)
    upper2 = jnp.concatenate([upper, upper], 1)
    lower = ones_where(row > col)
    lower2 = jnp.concatenate([lower, lower], 1)
    lane = lax.broadcasted_iota(jnp.int32, db_acc.shape, 1)
    at = range(len(hs))
    kus = [unit(k_ref[:, columns(h)].astype(F32)) for h in hs]
    betas, grows, tails = ([keep[x][h] for h in hs] for x in ("beta", "growth", "tail"))
    fss = [split(keep["fin"][h]) for h in hs]
    tks = [ku[0] * tail for ku, tail in zip(kus, tails)]
    dnews = [keep["pc"][h] + mm(split(tk), fs, "nt") for h, tk, fs in zip(hs, tks, fss)]
    nss = [split(keep["wv"][h]) for h in hs]
    errs = [mm(split(keep["inv"][h]), split(dnew), "tn") for h, dnew in zip(hs, dnews)]
    dtks = [mm(ns, fs, "nn") for ns, fs in zip(nss, fss)]
    ess = [split(err) for err in errs]
    dlows = [jnp.where(row > col, -mm(es, ns, "nt"), 0.0) for es, ns in zip(ess, nss)]
    dkws = [-mm(es, split(keep["st"][h]), "nt") for es, h in zip(ess, hs)]
    b2s = [split(dlows[j] * betas[j] * keep["pair"][h]) for j, h in enumerate(hs)]
    kss = [split(ku[0]) for ku in kus]
    kgs = [g * d for g, d in zip(grows, dkws)]
    dkns = [
        keep["wk"][h] + mm(b2s[j], kss[j], "nn") + mm(b2s[j], kss[j], "tn")
        + betas[j] * kgs[j] + tails[j] * dtks[j]
        for j, h in enumerate(hs)
    ]
    dlgs = [dlows[j] * keep["gram"][h] for j, h in enumerate(hs)]
    kgs = [ku[0] * kg for ku, kg in zip(kus, kgs)]
    ups = [
        dot(upper2, jnp.concatenate(split(jnp.concatenate(
            [keep["z"][h] + betas[j] * dlgs[j], keep["x"][h] + betas[j] * kgs[j]], 1
        )), 0), "nn")
        for j, h in enumerate(hs)
    ]
    belows = [
        dot(lower2, jnp.concatenate(split(dtk * tk), 0), "nn") for dtk, tk in zip(dtks, tks)
    ]
    dks = [
        (kr * (dkn - kn * jnp.sum(dkn * kn, axis=1, keepdims=True))).astype(BF)
        for (kn, kr), dkn in zip(kus, dkns)
    ]
    dbetas = [
        jnp.sum(
            (dlgs[j] + kgs[j] + errs[j] * v_ref[:, columns(h)].astype(F32))
            * (betas[j] * (1.0 - betas[j])), axis=1, keepdims=True,
        )
        for j, h in enumerate(hs)
    ]
    totals = [
        jnp.sum(
            jnp.sum(keep["st"][h] * keep["fin"][h].T * grows[j][C - 1 :, :], axis=1, keepdims=True),
            axis=0, keepdims=True,
        )
        for j, h in enumerate(hs)
    ]
    dgates = [
        totals[j] + jnp.sum(
            jnp.where(row > col, ups[j][:, :C], 0.0) + ups[j][:, C:] + belows[j],
            axis=1, keepdims=True,
        )
        for j in at
    ]
    db, dg = db_acc[...], dg_acc[...]
    for j, h in enumerate(hs):
        dk_ref[:, columns(h)] = dks[j]
        dv_ref[:, columns(h)] = (betas[j] * errs[j]).astype(BF)
        db, dg = jnp.where(lane == h, dbetas[j], db), jnp.where(lane == h, dgates[j], dg)
    db_acc[...] = db
    dg_acc[...] = dg


KEPT = (
    "inv", "wk", "wv", "pc", "beta", "growth", "tail",
    "pair", "scores", "gram", "z", "x", "st", "fin",
)
OWN = ("roe", "sin", "sout", "sgive", "dz", "dp", "eout", "fgive")
TWICE = ("aup", "xin", "xout", "pin")
SENDS = ("state", "pack", "up", "mid", "down", "pair", "near", "far", "relay", "fin")
RECVS = ("state", "pack", "mid", "down", "pair", "far", "relay", "fin")
QUAD, DUO = 4, 2
STEPS, HOP = 3, 2


def pair_of(ref, k):
    return ref[k, :, :D], ref[k, :, D:]


def chain_kernel(
    heads, n, n_outer,
    b_ref, g_ref, q_ref, k_ref, v_ref, c_ref, s0_ref,
    dq_ref, dk_ref, dv_ref, db_ref, dg_ref,
    *scratch,
):
    args = (b_ref, g_ref, q_ref, k_ref, v_ref, c_ref)
    scratch = list(scratch)
    keep = {x: scratch.pop(0) for x in KEPT}
    roe, sin, sout, sgive, dz, dp, eout, fgive = (scratch.pop(0) for _ in OWN)
    aup, xin, xout, pin = (scratch.pop(0) for _ in TWICE)
    pack, both, db_acc, dg_acc = (scratch.pop(0) for _ in range(4))
    send = {x: scratch.pop(0) for x in SENDS}
    recv = {x: scratch.pop(0) for x in RECVS}
    st, fin = keep["st"], keep["fin"]
    o, i = lax.axis_index("outer"), lax.axis_index("inner")
    z, c = i // 2, lax.rem(i, 2)
    chips, own, quads = n // 2, heads // 2, heads // QUAD
    hpd = s0_ref.shape[0]
    top = z == chips - 1
    final_block = o == n_outer - 1
    even = lax.rem(o, 2) == 0
    barrier = pltpu.get_barrier_semaphore()
    for d in range(1, n):
        pl.semaphore_signal(
            barrier, inc=1, device_id=(o, lax.rem(i + d, n)), device_id_type=MESH
        )
    for d in range(1, n_outer):
        pl.semaphore_signal(
            barrier, inc=1, device_id=(lax.rem(o + d, n_outer), i), device_id_type=MESH
        )
    pl.semaphore_wait(barrier, n + n_outer - 2)

    def remote(src, dst, give, take, k, target):
        return pltpu.make_async_remote_copy(
            src_ref=src, dst_ref=dst, send_sem=send[give].at[k], recv_sem=recv[take].at[k],
            device_id=target, device_id_type=MESH,
        )

    mate = (o, i + 1 - 2 * c)
    above = (o, lax.rem(i + 2, n))
    below = (o, lax.rem(i + n - 2, n))
    before = (lax.rem(o + n_outer - 1, n_outer), i)
    before2 = (lax.rem(o + n_outer - 2, n_outer), i)

    def pack_copy(k):
        h = 2 * k + 1 - c
        return remote(pack.at[0, h], pack.at[1, h], "pack", "pack", k, mate)

    def up_copy(k):
        return remote(sout.at[k], sin.at[k], "up", "state", k, above)

    def mid_copy(k):
        return remote(sgive.at[k], st.at[2 * k + c], "mid", "mid", k, mate)

    def down_copy(k):
        return remote(xout.at[k], xin.at[k], "down", "down", k, below)

    def pair_copy(k):
        return remote(xout.at[k], pin.at[k], "pair", "pair", k, before)

    def near_copy(k):
        return remote(eout.at[k], dz.at[k], "near", "relay", k, before)

    def far_copy(k):
        return remote(eout.at[k], dp.at[k], "far", "far", k, before2)

    def relay_copy(k):
        return remote(dz.at[k], dz.at[k], "relay", "relay", k, above)

    def fin_copy(k):
        return remote(fgive.at[k], fin.at[2 * k + c], "fin", "fin", k, mate)

    for j in range(hpd):
        h = i * hpd + j
        k, owner = h // 2, lax.rem(h, 2)

        @pl.when(i == owner)
        def _():
            pltpu.make_async_copy(s0_ref.at[j], sin.at[k], recv["state"].at[k]).start()

        @pl.when(i != owner)
        def _():
            pltpu.make_async_remote_copy(
                src_ref=s0_ref.at[j], dst_ref=sin.at[k], send_sem=send["state"].at[j],
                recv_sem=recv["state"].at[k], device_id=(o, owner), device_id_type=MESH,
            ).start()

    db_acc[...] = jnp.zeros_like(db_acc)
    dg_acc[...] = jnp.zeros_like(dg_acc)

    @pl.when(final_block)
    def _():
        dz[...] = jnp.zeros_like(dz)

    @pl.when((o == n_outer - 2) & (z == 0))
    def _():
        dp[...] = jnp.zeros_like(dp)

    @pl.when(top)
    def _():
        row, col = iotas()
        ident = jnp.where(row == col, 1.0, 0.0)
        for k in range(own):
            xin[k] = jnp.concatenate([jnp.zeros_like(ident), ident], 0)

    lag_down = HOP * (chips - 1 - z)
    lag_outer = jnp.where(final_block, 0, HOP * (n_outer // 2 - o // 2))
    lag_d = HOP * (chips - 1) + lag_outer + HOP * z
    lag_d = jnp.where(final_block, lag_down, lag_d)

    def start_of(k):
        return STEPS * (k // 2) + lax.rem(k, 2) + STEPS

    def at(t, lag):
        late = t - lag - STEPS
        k = 2 * (late // STEPS) + lax.rem(late, STEPS)
        ok = (late >= 0) & (lax.rem(late, STEPS) < 2) & (k < own)
        return ok, jnp.where(ok, k, own)

    heavy = STEPS * quads
    last_start = STEPS * ((own - 1) // 2) + (own - 1) % 2 + STEPS
    state_base = jnp.maximum(heavy, last_start + HOP * z + 1 - (own - 1))
    ticks = jnp.maximum(state_base + 1 + own, last_start + lag_d + 2)
    ticks = jnp.maximum(ticks, state_base + own + own)

    def grad_tick(j):
        return jnp.maximum(state_base + own + j, start_of(j) + lag_d + 1)

    def combine(k):
        h = 2 * k + c

        def part(slot):
            return pack[slot, h, 0], pack[slot, h, 1], pack[slot, h, 2]

        me, ae, re = part(c)
        mo, ao, ro = part(1 - c)
        mes = split(me)
        both_rows = mm(split(jnp.concatenate([mo, ro], 0)), mes, "nn")
        joined = both_rows[:D]
        back = both_rows[D:] + re
        aoe = mm(split(mo), split(ae), "nn") + ao
        both[k] = jnp.concatenate(
            [jnp.concatenate(split(joined), 1), jnp.concatenate(mes, 1)], 0
        )
        aup[k] = jnp.concatenate([aoe, ae], 0)
        roe[k] = back

        @pl.when(top)
        def _():
            xout[k] = jnp.concatenate([back, joined], 0)

    def tick(t, carry):
        q, step = t // STEPS, lax.rem(t, STEPS)
        in_group = t < heavy

        @pl.when(in_group & (step == 0))
        def _():
            group_start([q * QUAD + s for s in range(QUAD)], args, keep)

        @pl.when(in_group & (step == 1))
        def _():
            group_solve([q * QUAD + s for s in range(QUAD)], keep)

        @pl.when(in_group & (step == 2))
        def _():
            group_end([q * QUAD + s for s in range(QUAD)], args, keep, pack)
            for s in range(2):
                pack_copy(2 * q + s).start()

        j = t - state_base

        @pl.when((j >= 0) & (j < own))
        def _():
            mid_copy(j).wait_recv()
            state_stage([2 * j, 2 * j + 1], args, keep, dq_ref)

        j = jnp.int32(0)
        for jj in range(own):
            j += (grad_tick(jj) < t).astype(jnp.int32)

        @pl.when((j < own) & (grad_tick(j) == t))
        def _():
            fin_copy(j).wait_recv()
            grad_stage([2 * j, 2 * j + 1], args, keep, dk_ref, dv_ref, db_acc, dg_acc)

        ok, kc = at(t, 0)

        @pl.when(ok)
        def _():
            pack_copy(kc).wait_recv()
            combine(kc)

            @pl.when(top)
            def _():
                down_copy(kc).start()

        up_ok, ku = at(t, HOP * z)
        down_ok, kd = at(t, lag_down)
        down_ok = down_ok & jnp.logical_not(top)
        kd = jnp.where(down_ok, kd, own)

        @pl.when(up_ok)
        def _():
            pltpu.make_async_copy(sin.at[ku], sin.at[ku], recv["state"].at[ku]).wait()

        @pl.when(down_ok)
        def _():
            down_copy(kd).wait_recv()

        @pl.when(up_ok | down_ok)
        def _():
            state = sin[ku]
            moved = mm(pair_of(both, ku), split(state), "nn") + aup[ku]
            wide = both[kd, :D, :]
            back = mm(split(xin[kd]), (wide[:, :D], wide[:, D:]), "nn")
            sout[ku] = moved[:D]
            mid = moved[D:]
            hs = 2 * ku + c
            st[hs] = jnp.where(c == 0, state, mid)
            sgive[ku] = jnp.where(c == 0, mid, state)
            xout[kd] = jnp.concatenate([back[:D] + roe[kd], back[D:]], 0)

        @pl.when(up_ok)
        def _():
            @pl.when(jnp.logical_not(top))
            def _():
                up_copy(ku).start()

            mid_copy(ku).start()

        @pl.when(down_ok & (z > 0))
        def _():
            down_copy(kd).start()

        @pl.when(down_ok & (z == 0) & jnp.logical_not(even))
        def _():
            pair_copy(kd).start()

        d_ok, k = at(t, lag_d)

        @pl.when(d_ok & (z == 0) & even)
        def _():
            pair_copy(k).wait_recv()

            @pl.when(o < n_outer - 2)
            def _():
                far_copy(k).wait_recv()

            end = pin[k, :D, :] + mm(split(dp[k]), split(pin[k, D:, :]), "nn")
            dz[k] = end

            @pl.when(o > 0)
            def _():
                eout[k] = xout[k, :D, :] + mm(split(end), split(xout[k, D:, :]), "nn")
                near_copy(k).start()
                far_copy(k).start()

        @pl.when(d_ok & jnp.logical_not(final_block))
        def _():
            @pl.when((z > 0) | jnp.logical_not(even))
            def _():
                relay_copy(k).wait_recv()

            @pl.when(jnp.logical_not(top))
            def _():
                relay_copy(k).start()

        @pl.when(d_ok)
        def _():
            h = 2 * k + c
            odd_end = xin[k, :D, :] + mm(split(dz[k]), split(xin[k, D:, :]), "nn")
            even_end = pack[1 - c, h, 2] + mm(split(odd_end), split(pack[1 - c, h, 0]), "nn")
            fin[h] = jnp.where(c == 0, even_end, odd_end)
            fgive[k] = jnp.where(c == 0, odd_end, even_end)
            fin_copy(k).start()

        return carry

    lax.fori_loop(0, ticks, tick, 0)
    db_ref[...] = db_acc[...].T[:heads].astype(BF)
    dg_ref[...] = dg_acc[...].T[:heads].astype(BF)

    for j in range(hpd):
        h = i * hpd + j
        owner = lax.rem(h, 2)

        @pl.when(i != owner)
        def _():
            pltpu.make_async_remote_copy(
                src_ref=s0_ref.at[j], dst_ref=sin.at[h // 2], send_sem=send["state"].at[j],
                recv_sem=recv["state"].at[h // 2], device_id=(o, owner), device_id_type=MESH,
            ).wait_send()

    def finish(k, carry):
        pack_copy(k).wait_send()
        mid_copy(k).wait_send()
        fin_copy(k).wait_send()

        @pl.when(jnp.logical_not(top))
        def _():
            up_copy(k).wait_send()

        @pl.when(z > 0)
        def _():
            down_copy(k).wait_send()

        @pl.when((z == 0) & jnp.logical_not(even))
        def _():
            pair_copy(k).wait_send()

        @pl.when((z == 0) & even & (o > 0))
        def _():
            near_copy(k).wait_send()
            far_copy(k).wait_send()

        @pl.when(jnp.logical_not(top) & jnp.logical_not(final_block))
        def _():
            relay_copy(k).wait_send()

        return carry

    lax.fori_loop(0, own, finish, 0)


def shards(n, n_outer, queries, key_rows, value_rows, beta_logit, log_gate, out_grad, block_states):
    heads = beta_logit.shape[1]
    own = heads // 2
    big = jax.ShapeDtypeStruct(queries.shape, BF)
    thin = jax.ShapeDtypeStruct((heads, C), BF)
    acc = pltpu.VMEM((C, D), F32)
    sems = pltpu.SemaphoreType.DMA((own,))
    dq, dk, dv, db, dg = pl.pallas_call(
        functools.partial(chain_kernel, heads, n, n_outer),
        out_shape=(big, big, big, thin, thin),
        in_specs=[VM] * 7,
        out_specs=(VM,) * 5,
        scratch_shapes=[pltpu.VMEM((heads + 2, D, D), F32)] * len(KEPT)
        + [pltpu.VMEM((own + 1, D, D), F32)] * len(OWN)
        + [pltpu.VMEM((own + 1, 2 * D, D), F32)] * len(TWICE)
        + [pltpu.VMEM((2, heads, 3, D, D), F32), pltpu.VMEM((own + 1, 2 * D, 2 * D), BF), acc, acc]
        + [sems] * (len(SENDS) + len(RECVS)),
        compiler_params=pltpu.CompilerParams(
            vmem_limit_bytes=56 << 20, collective_id=0, has_side_effects=True
        ),
    )(beta_logit.T, log_gate.T, queries, key_rows, value_rows, out_grad, block_states[0])
    return dq, dk, dv, db.T, dg.T


def solution(mesh):
    wide = P(("outer", "inner"), None)
    return jax.shard_map(
        functools.partial(shards, mesh.shape["inner"], mesh.shape["outer"]),
        mesh=mesh,
        in_specs=(wide,) * 6 + (P("outer", "inner", None, None),),
        out_specs=(wide,) * 5,
        check_vma=False,
    )
```

```python
import functools

import jax
import jax.numpy as jnp
from jax import lax
from jax.experimental import pallas as pl
from jax.experimental.pallas import tpu as pltpu
from jax.sharding import PartitionSpec as P

D = 128
C = 128
BF = jnp.bfloat16
F32 = jnp.float32
MESH = pl.DeviceIdType.MESH
VM = pl.BlockSpec(memory_space=pltpu.VMEM)
DIMS = {"nn": ((1,), (0,)), "nt": ((1,), (1,)), "tn": ((0,), (0,))}


def split(x):
    hi = x.astype(BF)
    return hi, (x - hi.astype(F32)).astype(BF)


def exact(x):
    return x.astype(BF), None


def dot(a, b, mode):
    return lax.dot_general(a, b, (DIMS[mode], ((), ())), preferred_element_type=F32)


def mm(a, b, mode):
    ka = 0 if mode == "tn" else 1
    kb = 1 if mode == "nt" else 0
    (ah, al), (bh, bl) = a, b
    if al is None and bl is None:
        return dot(ah, bh, mode)
    if al is None:
        return dot(jnp.concatenate([ah, ah], ka), jnp.concatenate([bh, bl], kb), mode)
    left = jnp.concatenate([ah, al], ka)
    if bl is None:
        return dot(left, jnp.concatenate([bh, bh], kb), mode)
    top = jnp.concatenate([bh, bl], 1 - kb)
    low = jnp.concatenate([bh, jnp.zeros_like(bl)], 1 - kb)
    both = dot(left, jnp.concatenate([top, low], kb), mode)
    n = both.shape[1] // 2
    return both[:, :n] + both[:, n:]


def iotas():
    return lax.broadcasted_iota(jnp.int32, (C, C), 0), lax.broadcasted_iota(jnp.int32, (C, C), 1)


def ones_where(mask):
    return jnp.where(mask, 1.0, 0.0).astype(BF)


def unit(x):
    r = lax.rsqrt(jnp.sum(x * x, axis=1, keepdims=True) + 1e-06)
    return x * r, r


def decays(gate, row, col):
    wide = gate
    rhs = jnp.concatenate([wide, jnp.where(row > col, wide, 0.0)], 1).astype(BF)
    both = dot(ones_where(row >= col), rhs, "nn")
    after = dot(ones_where(row < col), wide.astype(BF), "nn")
    pair = jnp.where(row >= col, jnp.exp(both[:, C:]), 0.0)
    return jnp.exp(both[:, :C]), jnp.exp(after), pair


def inverses(lowers, row, col):
    eye = jnp.where(row == col, 1.0, 0.0)
    done = [eye - jnp.where((row // 2 == col // 2), low, 0.0) for low in lowers]
    size = 2
    while size < C:
        pick = (row // (2 * size) == col // (2 * size)) & (row // size != col // size)
        halves = [split(t) for t in done]
        mids = [mm(t, split(jnp.where(pick, low, 0.0)), "nn") for t, low in zip(halves, lowers)]
        done = [t - mm(split(m), h, "nn") for t, m, h in zip(done, mids, halves)]
        size *= 2
    return done


def head_columns(b_ref, g_ref, h):
    heads = b_ref.shape[0]
    pick = ones_where(lax.broadcasted_iota(jnp.int32, (heads, C), 0) == h)
    return jax.nn.sigmoid(dot(b_ref[...], pick, "tn")), dot(g_ref[...], pick, "tn")


def grams(qn, kn, pair, row, col):
    qs, ks = split(qn), split(kn)
    left = (jnp.concatenate([qs[0], ks[0]], 0), jnp.concatenate([qs[1], ks[1]], 0))
    both = mm(left, ks, "nt")
    return both[:C] * pair, jnp.where(row > col, both[C:] * pair, 0.0)


def columns(h):
    return pl.ds(pl.multiple_of(h * D, D), D)


def group_start(hs, args, keep):
    b_ref, g_ref, q_ref, k_ref, _, c_ref = args
    row, col = iotas()
    cols = [head_columns(b_ref, g_ref, h) for h in hs]
    qns = [unit(q_ref[:, columns(h)].astype(F32))[0] for h in hs]
    kns = [unit(k_ref[:, columns(h)].astype(F32))[0] for h in hs]
    decs = [decays(gate, row, col) for _, gate in cols]
    gms = [grams(qn, kn, pair, row, col) for qn, kn, (_, _, pair) in zip(qns, kns, decs)]
    cots = [exact(c_ref[:, columns(h)]) for h in hs]
    qparts = [mm(cot, split(qn * d[0]), "tn") for cot, qn, d in zip(cots, qns, decs)]
    pcs = [mm(split(scores), cot, "tn") for (scores, _), cot in zip(gms, cots)]
    for j, h in enumerate(hs):
        for name, value in (
            ("beta", cols[j][0]), ("growth", decs[j][0]), ("tail", decs[j][1]),
            ("pair", decs[j][2]), ("scores", gms[j][0]), ("gram", gms[j][1]),
            ("pc", pcs[j]), ("x", qparts[j]),
        ):
            keep[name][h] = value


def group_solve(hs, keep):
    row, col = iotas()
    lowers = [keep["beta"][h] * keep["gram"][h] for h in hs]
    for h, inv in zip(hs, inverses(lowers, row, col)):
        keep["inv"][h] = inv


def group_end(hs, args, keep, pack):
    _, _, _, k_ref, v_ref, _ = args
    row, col = iotas()
    eye = row == col
    kns = [unit(k_ref[:, columns(h)].astype(F32))[0] for h in hs]
    betas = [keep["beta"][h] for h in hs]
    grows = [keep["growth"][h] for h in hs]
    invs = [split(keep["inv"][h]) for h in hs]
    wks = [mm(i, split(b * g * kn), "nn") for i, b, g, kn in zip(invs, betas, grows, kns)]
    wvs = [
        mm(i, split(b * v_ref[:, columns(h)].astype(F32)), "nn")
        for i, b, h in zip(invs, betas, hs)
    ]
    tss = [split(kn * keep["tail"][h]) for kn, h in zip(kns, hs)]
    wss = [split(wk) for wk in wks]
    lasts = [jnp.where(eye, jnp.broadcast_to(g[C - 1 :, :], (C, C)), 0.0) for g in grows]
    ms = [last - mm(ts, ws, "tn") for last, ts, ws in zip(lasts, tss, wss)]
    rs = [keep["x"][h] - mm(split(keep["pc"][h]), ws, "tn") for h, ws in zip(hs, wss)]
    ads = [mm(ts, split(wv), "tn") for ts, wv in zip(tss, wvs)]
    for j, h in enumerate(hs):
        keep["wk"][h] = wks[j]
        keep["wv"][h] = wvs[j]
        pack[0, h, 0] = ms[j]
        pack[0, h, 1] = ads[j]
        pack[0, h, 2] = rs[j]


def state_stage(hs, args, keep, dq_ref):
    _, _, q_ref, k_ref, _, c_ref = args
    qus = [unit(q_ref[:, columns(h)].astype(F32)) for h in hs]
    kns = [unit(k_ref[:, columns(h)].astype(F32))[0] for h in hs]
    cots = [exact(c_ref[:, columns(h)]) for h in hs]
    sss = [split(keep["st"][h]) for h in hs]
    news = [keep["wv"][h] - mm(split(keep["wk"][h]), ss, "nn") for h, ss in zip(hs, sss)]
    dqgs = [keep["growth"][h] * mm(cot, ss, "nt") for h, cot, ss in zip(hs, cots, sss)]
    dscs = [mm(cot, split(new), "nt") for cot, new in zip(cots, news)]
    b1s = [split(dsc * keep["pair"][h]) for h, dsc in zip(hs, dscs)]
    dqns = [mm(b1, split(kn), "nn") + dqg for b1, kn, dqg in zip(b1s, kns, dqgs)]
    wks = [mm(b1, split(qn), "tn") for b1, (qn, _) in zip(b1s, qus)]
    dqs = [
        (qr * (dqn - qn * jnp.sum(dqn * qn, axis=1, keepdims=True))).astype(BF)
        for (qn, qr), dqn in zip(qus, dqns)
    ]
    zs = [dsc * keep["scores"][h] for h, dsc in zip(hs, dscs)]
    for j, h in enumerate(hs):
        dq_ref[:, columns(h)] = dqs[j]
        keep["wv"][h] = news[j]
        keep["wk"][h] = wks[j]
        keep["z"][h] = zs[j]
        keep["x"][h] = dqgs[j] * qus[j][0]


def grad_stage(hs, args, keep, dk_ref, dv_ref, db_acc, dg_acc):
    _, _, _, k_ref, v_ref, _ = args
    row, col = iotas()
    upper = ones_where(row <= col)
    upper2 = jnp.concatenate([upper, upper], 1)
    lower = ones_where(row > col)
    lower2 = jnp.concatenate([lower, lower], 1)
    lane = lax.broadcasted_iota(jnp.int32, db_acc.shape, 1)
    at = range(len(hs))
    kus = [unit(k_ref[:, columns(h)].astype(F32)) for h in hs]
    betas, grows, tails = ([keep[x][h] for h in hs] for x in ("beta", "growth", "tail"))
    fss = [split(keep["fin"][h]) for h in hs]
    tks = [ku[0] * tail for ku, tail in zip(kus, tails)]
    dnews = [keep["pc"][h] + mm(split(tk), fs, "nt") for h, tk, fs in zip(hs, tks, fss)]
    nss = [split(keep["wv"][h]) for h in hs]
    errs = [mm(split(keep["inv"][h]), split(dnew), "tn") for h, dnew in zip(hs, dnews)]
    dtks = [mm(ns, fs, "nn") for ns, fs in zip(nss, fss)]
    ess = [split(err) for err in errs]
    dlows = [jnp.where(row > col, -mm(es, ns, "nt"), 0.0) for es, ns in zip(ess, nss)]
    dkws = [-mm(es, split(keep["st"][h]), "nt") for es, h in zip(ess, hs)]
    b2s = [split(dlows[j] * betas[j] * keep["pair"][h]) for j, h in enumerate(hs)]
    kss = [split(ku[0]) for ku in kus]
    kgs = [g * d for g, d in zip(grows, dkws)]
    dkns = [
        keep["wk"][h] + mm(b2s[j], kss[j], "nn") + mm(b2s[j], kss[j], "tn")
        + betas[j] * kgs[j] + tails[j] * dtks[j]
        for j, h in enumerate(hs)
    ]
    dlgs = [dlows[j] * keep["gram"][h] for j, h in enumerate(hs)]
    kgs = [ku[0] * kg for ku, kg in zip(kus, kgs)]
    ups = [
        dot(upper2, jnp.concatenate(split(jnp.concatenate(
            [keep["z"][h] + betas[j] * dlgs[j], keep["x"][h] + betas[j] * kgs[j]], 1
        )), 0), "nn")
        for j, h in enumerate(hs)
    ]
    belows = [
        dot(lower2, jnp.concatenate(split(dtk * tk), 0), "nn") for dtk, tk in zip(dtks, tks)
    ]
    dks = [
        (kr * (dkn - kn * jnp.sum(dkn * kn, axis=1, keepdims=True))).astype(BF)
        for (kn, kr), dkn in zip(kus, dkns)
    ]
    dbetas = [
        jnp.sum(
            (dlgs[j] + kgs[j] + errs[j] * v_ref[:, columns(h)].astype(F32))
            * (betas[j] * (1.0 - betas[j])), axis=1, keepdims=True,
        )
        for j, h in enumerate(hs)
    ]
    totals = [
        jnp.sum(
            jnp.sum(keep["st"][h] * keep["fin"][h].T * grows[j][C - 1 :, :], axis=1, keepdims=True),
            axis=0, keepdims=True,
        )
        for j, h in enumerate(hs)
    ]
    dgates = [
        totals[j] + jnp.sum(
            jnp.where(row > col, ups[j][:, :C], 0.0) + ups[j][:, C:] + belows[j],
            axis=1, keepdims=True,
        )
        for j in at
    ]
    db, dg = db_acc[...], dg_acc[...]
    for j, h in enumerate(hs):
        dk_ref[:, columns(h)] = dks[j]
        dv_ref[:, columns(h)] = (betas[j] * errs[j]).astype(BF)
        db, dg = jnp.where(lane == h, dbetas[j], db), jnp.where(lane == h, dgates[j], dg)
    db_acc[...] = db
    dg_acc[...] = dg


KEPT = (
    "inv", "wk", "wv", "pc", "beta", "growth", "tail",
    "pair", "scores", "gram", "z", "x", "st", "fin",
)
OWN = ("sin", "sout", "sgive", "dz", "dp", "eout", "fgive", "vout")
TWICE = ("aup", "xout", "pin")
SENDS = ("state", "pack", "up", "mid", "down", "pair", "near", "far", "relay", "fin")
RECVS = ("state", "pack", "mid", "down", "pair", "far", "relay", "fin")
QUAD, DUO = 4, 2
STEPS = 3
HOP_UP, HOP, HOP_OUT, HOP_BACK = 3, 2, 3, 3
LATE_UP = 0


def pair_of(ref, k):
    return ref[k, :, :D], ref[k, :, D:]


def chain_kernel(
    heads, n, n_outer,
    b_ref, g_ref, q_ref, k_ref, v_ref, c_ref, s0_ref,
    dq_ref, dk_ref, dv_ref, db_ref, dg_ref,
    *scratch,
):
    args = (b_ref, g_ref, q_ref, k_ref, v_ref, c_ref)
    scratch = list(scratch)
    keep = {x: scratch.pop(0) for x in KEPT}
    sin, sout, sgive, dz, dp, eout, fgive, vout = (scratch.pop(0) for _ in OWN)
    aup, xout, pin = (scratch.pop(0) for _ in TWICE)
    pack, duo, both, db_acc, dg_acc = (scratch.pop(0) for _ in range(5))
    send = {x: scratch.pop(0) for x in SENDS}
    recv = {x: scratch.pop(0) for x in RECVS}
    st, fin = keep["st"], keep["fin"]
    o, i = lax.axis_index("outer"), lax.axis_index("inner")
    z, c = i // 2, lax.rem(i, 2)
    chips, own, quads = n // 2, heads // 2, heads // QUAD
    hpd = s0_ref.shape[0]
    top = z == chips - 1
    zz = jnp.where(c == 0, z, chips - 1 - z)
    root, leaf = zz == 0, zz == chips - 1
    final_block = o == n_outer - 1
    even = lax.rem(o, 2) == 0
    barrier = pltpu.get_barrier_semaphore()
    for d in range(1, n):
        pl.semaphore_signal(
            barrier, inc=1, device_id=(o, lax.rem(i + d, n)), device_id_type=MESH
        )
    for d in range(1, n_outer):
        pl.semaphore_signal(
            barrier, inc=1, device_id=(lax.rem(o + d, n_outer), i), device_id_type=MESH
        )

    def remote(src, dst, give, take, k, target):
        return pltpu.make_async_remote_copy(
            src_ref=src, dst_ref=dst, send_sem=send[give].at[k], recv_sem=recv[take].at[k],
            device_id=target, device_id_type=MESH,
        )

    mate = (o, i + 1 - 2 * c)
    above = (o, lax.rem(i + 2, n))
    inward = (o, lax.rem(i + n - 2 + 4 * c, n))
    outward = (o, lax.rem(i + n + 2 - 4 * c, n))
    before = (lax.rem(o + n_outer - 1, n_outer), i)
    before2 = (lax.rem(o + n_outer - 2, n_outer), i)

    def pack_copy(k):
        h = 2 * k + 1 - c
        return remote(pack.at[0, h], pack.at[1, h], "pack", "pack", k, mate)

    def up_copy(k):
        return remote(sout.at[k], sin.at[k], "up", "state", k, above)

    def mid_copy(k):
        return remote(sgive.at[k], st.at[2 * k + c], "mid", "mid", k, mate)

    def down_copy(k):
        return remote(xout.at[k], duo.at[0, k], "down", "down", k, inward)

    def pair_copy(k):
        return remote(xout.at[k], pin.at[k], "pair", "pair", k, before)

    def near_copy(k):
        return remote(eout.at[k], dz.at[k], "near", "relay", k, before)

    def far_copy(k):
        return remote(eout.at[k], dp.at[k], "far", "far", k, before2)

    def relay_copy(k):
        return remote(dz.at[k], dz.at[k], "relay", "relay", k, outward)

    def pass_copy(k):
        return remote(vout.at[k], dz.at[k], "relay", "relay", k, outward)

    def fin_copy(k):
        return remote(fgive.at[k], fin.at[2 * k + c], "fin", "fin", k, mate)

    for j in range(hpd):
        h = i * hpd + j

        @pl.when(i == lax.rem(h, 2))
        def _():
            k = h // 2
            pltpu.make_async_copy(s0_ref.at[j], sin.at[k], recv["state"].at[k]).start()

    def begin():
        pl.semaphore_wait(barrier, n + n_outer - 2)
        for j in range(hpd):
            h = i * hpd + j
            owner = lax.rem(h, 2)

            @pl.when(i != owner)
            def _():
                pltpu.make_async_remote_copy(
                    src_ref=s0_ref.at[j], dst_ref=sin.at[h // 2], send_sem=send["state"].at[j],
                    recv_sem=recv["state"].at[h // 2], device_id=(o, owner), device_id_type=MESH,
                ).start()

    db_acc[...] = jnp.zeros_like(db_acc)
    dg_acc[...] = jnp.zeros_like(dg_acc)

    @pl.when(final_block & ((c == 0) | root))
    def _():
        dz[...] = jnp.zeros_like(dz)

    @pl.when((o == n_outer - 2) & root)
    def _():
        dp[...] = jnp.zeros_like(dp)

    @pl.when(leaf)
    def _():
        row, col = iotas()
        ident = jnp.where(row == col, 1.0, 0.0)
        for k in range(own):
            duo[0, k] = jnp.concatenate([jnp.zeros_like(ident), ident], 0)

    relays = jnp.logical_not(leaf) & (jnp.logical_not(final_block) | (c == 1))
    landing = jnp.where(root, jnp.logical_not(even | final_block), jnp.logical_not(final_block) | (c == 1))
    lag_down = HOP * (chips - 1 - zz)
    lag_root = HOP * (chips - 1) + HOP_OUT * (n_outer // 2 - o // 2)
    ends = [
        jnp.where(final_block, HOP * (chips - 1 - z), lag_root + HOP_BACK * z),
        jnp.where(final_block, 0, lag_root) + HOP_BACK * (chips - 1 - z),
    ]
    lag_d = jnp.where(c == 0, ends[0], ends[1])
    lag_both = jnp.maximum(ends[0], ends[1])
    lag_up = LATE_UP + HOP_UP * z

    def start_of(k):
        return STEPS * (k // 2) + lax.rem(k, 2) + STEPS

    def at(t, lag):
        late = t - lag - STEPS
        k = 2 * (late // STEPS) + lax.rem(late, STEPS)
        ok = (late >= 0) & (lax.rem(late, STEPS) < 2) & (k < own)
        return ok, jnp.where(ok, k, own)

    heavy = STEPS * quads
    last_start = STEPS * ((own - 1) // 2) + (own - 1) % 2 + STEPS
    state_base = jnp.maximum(heavy, last_start + lag_up + 1 - (own - 1))
    ticks = jnp.maximum(state_base + 1 + own, last_start + lag_both + 2)
    ticks = jnp.maximum(ticks, state_base + own + own)

    def grad_tick(j):
        return jnp.maximum(state_base + own + j, start_of(j) + lag_both + 1)

    def combine(k):
        h = 2 * k + c

        def part(slot):
            return pack[slot, h, 0], pack[slot, h, 1], pack[slot, h, 2]

        me, ae, re = part(c)
        mo, ao, ro = part(1 - c)
        mes = split(me)
        both_rows = mm(split(jnp.concatenate([mo, ro], 0)), mes, "nn")
        joined = both_rows[:D]
        back = both_rows[D:] + re
        aoe = mm(split(mo), split(ae), "nn") + ao
        both[k] = jnp.concatenate(
            [jnp.concatenate(split(joined), 1), jnp.concatenate(mes, 1)], 0
        )
        aup[k] = jnp.concatenate([aoe, ae], 0)
        whole = jnp.concatenate([back, joined], 0)
        duo[1, k] = whole

        @pl.when(leaf)
        def _():
            xout[k] = whole

    def tick(t, carry):
        q, step = t // STEPS, lax.rem(t, STEPS)
        in_group = t < heavy

        @pl.when(in_group & (step == 0))
        def _():
            group_start([q * QUAD + s for s in range(QUAD)], args, keep)

        @pl.when(in_group & (step == 1))
        def _():
            group_solve([q * QUAD + s for s in range(QUAD)], keep)

        @pl.when(in_group & (step == 2))
        def _():
            group_end([q * QUAD + s for s in range(QUAD)], args, keep, pack)

            @pl.when(t == STEPS - 1)
            def _():
                begin()

            for s in range(2):
                pack_copy(2 * q + s).start()

        j = t - state_base

        @pl.when((j >= 0) & (j < own))
        def _():
            mid_copy(j).wait_recv()
            state_stage([2 * j, 2 * j + 1], args, keep, dq_ref)

        j = jnp.int32(0)
        for jj in range(own):
            j += (grad_tick(jj) < t).astype(jnp.int32)

        @pl.when((j < own) & (grad_tick(j) == t))
        def _():
            fin_copy(j).wait_recv()
            grad_stage([2 * j, 2 * j + 1], args, keep, dk_ref, dv_ref, db_acc, dg_acc)

        ok, kc = at(t, 0)

        @pl.when(ok)
        def _():
            pack_copy(kc).wait_recv()
            combine(kc)

            @pl.when(leaf)
            def _():
                down_copy(kc).start()

        up_ok, ku = at(t, lag_up)
        down_ok, kd = at(t, lag_down)
        down_ok = down_ok & jnp.logical_not(leaf)
        kd = jnp.where(down_ok, kd, own)

        @pl.when(up_ok)
        def _():
            pltpu.make_async_copy(sin.at[ku], sin.at[ku], recv["state"].at[ku]).wait()

        @pl.when(down_ok)
        def _():
            down_copy(kd).wait_recv()

        @pl.when(up_ok | down_ok)
        def _():
            state = sin[ku]
            moved = mm(pair_of(both, ku), split(state), "nn") + aup[ku]
            near = duo[1 - c, kd]
            back = mm(split(duo[c, kd]), split(near[D:]), "nn")
            sout[ku] = moved[:D]
            mid = moved[D:]
            hs = 2 * ku + c
            st[hs] = jnp.where(c == 0, state, mid)
            sgive[ku] = jnp.where(c == 0, mid, state)
            xout[kd] = jnp.concatenate([back[:D] + near[:D], back[D:]], 0)

        @pl.when(up_ok)
        def _():
            @pl.when(jnp.logical_not(top))
            def _():
                up_copy(ku).start()

            mid_copy(ku).start()

        @pl.when(down_ok & jnp.logical_not(root))
        def _():
            down_copy(kd).start()

        @pl.when(down_ok & root & jnp.logical_not(even))
        def _():
            pair_copy(kd).start()

        d_ok, k = at(t, lag_d)

        @pl.when(d_ok & root & even)
        def _():
            pair_copy(k).wait_recv()

            @pl.when(o < n_outer - 2)
            def _():
                far_copy(k).wait_recv()

            end = pin[k, :D, :] + mm(split(dp[k]), split(pin[k, D:, :]), "nn")
            dz[k] = end

            @pl.when(o > 0)
            def _():
                eout[k] = xout[k, :D, :] + mm(split(end), split(xout[k, D:, :]), "nn")
                near_copy(k).start()
                far_copy(k).start()

        @pl.when(d_ok & landing)
        def _():
            relay_copy(k).wait_recv()

        @pl.when(d_ok & relays & (c == 0))
        def _():
            relay_copy(k).start()

        @pl.when(d_ok)
        def _():
            h = 2 * k + c
            end = dz[k]
            value = duo[c, k, :D, :] + mm(split(end), split(duo[c, k, D:, :]), "nn")

            @pl.when(relays & (c == 1))
            def _():
                vout[k] = value
                pass_copy(k).start()

            odd_end = jnp.where(c == 0, value, end)
            even_end = pack[1 - c, h, 2] + mm(split(odd_end), split(pack[1 - c, h, 0]), "nn")
            fin[h] = jnp.where(c == 0, even_end, odd_end)
            fgive[k] = jnp.where(c == 0, odd_end, even_end)
            fin_copy(k).start()

        return carry

    lax.fori_loop(0, ticks, tick, 0)
    db_ref[...] = db_acc[...].T[:heads].astype(BF)
    dg_ref[...] = dg_acc[...].T[:heads].astype(BF)

    for j in range(hpd):
        h = i * hpd + j
        owner = lax.rem(h, 2)

        @pl.when(i != owner)
        def _():
            pltpu.make_async_remote_copy(
                src_ref=s0_ref.at[j], dst_ref=sin.at[h // 2], send_sem=send["state"].at[j],
                recv_sem=recv["state"].at[h // 2], device_id=(o, owner), device_id_type=MESH,
            ).wait_send()

    def finish(k, carry):
        pack_copy(k).wait_send()
        mid_copy(k).wait_send()
        fin_copy(k).wait_send()

        @pl.when(jnp.logical_not(top))
        def _():
            up_copy(k).wait_send()

        @pl.when(jnp.logical_not(root))
        def _():
            down_copy(k).wait_send()

        @pl.when(root & jnp.logical_not(even))
        def _():
            pair_copy(k).wait_send()

        @pl.when(root & even & (o > 0))
        def _():
            near_copy(k).wait_send()
            far_copy(k).wait_send()

        @pl.when(relays)
        def _():
            relay_copy(k).wait_send()

        return carry

    lax.fori_loop(0, own, finish, 0)


def shards(n, n_outer, queries, key_rows, value_rows, beta_logit, log_gate, out_grad, block_states):
    heads = beta_logit.shape[1]
    own = heads // 2
    big = jax.ShapeDtypeStruct(queries.shape, BF)
    thin = jax.ShapeDtypeStruct((heads, C), BF)
    acc = pltpu.VMEM((C, D), F32)
    sems = pltpu.SemaphoreType.DMA((own,))
    dq, dk, dv, db, dg = pl.pallas_call(
        functools.partial(chain_kernel, heads, n, n_outer),
        out_shape=tuple(pltpu.VMEM(x.shape, x.dtype) for x in (big, big, big, thin, thin)),
        in_specs=[VM] * 7,
        out_specs=(VM,) * 5,
        scratch_shapes=[pltpu.VMEM((heads + 2, D, D), F32)] * len(KEPT)
        + [pltpu.VMEM((own + 1, D, D), F32)] * len(OWN)
        + [pltpu.VMEM((own + 1, 2 * D, D), F32)] * len(TWICE)
        + [
            pltpu.VMEM((2, heads, 3, D, D), F32),
            pltpu.VMEM((2, own + 1, 2 * D, D), F32),
            pltpu.VMEM((own + 1, 2 * D, 2 * D), BF),
            acc, acc,
        ]
        + [sems] * (len(SENDS) + len(RECVS)),
        compiler_params=pltpu.CompilerParams(
            vmem_limit_bytes=56 << 20, collective_id=0, has_side_effects=True
        ),
    )(beta_logit.T, log_gate.T, queries, key_rows, value_rows, out_grad, block_states[0])

    def hand_on(*refs):
        sem = refs[10]
        copies = [
            pltpu.make_async_copy(src, dst, sem.at[j])
            for j, (src, dst) in enumerate(zip(refs[:5], refs[5:10]))
        ]
        for copy in copies:
            copy.start()
        for copy in copies:
            copy.wait()

    dq, dk, dv, db, dg = pl.pallas_call(
        hand_on, out_shape=(big, big, big, thin, thin), in_specs=[VM] * 5,
        out_specs=(pl.BlockSpec(memory_space=pl.ANY),) * 5,
        scratch_shapes=[pltpu.SemaphoreType.DMA((5,))],
    )(*(pltpu.with_memory_space_constraint(x, pltpu.VMEM) for x in (dq, dk, dv, db, dg)))
    return dq, dk, dv, db.T, dg.T


def solution(mesh):
    wide = P(("outer", "inner"), None)
    return jax.shard_map(
        functools.partial(shards, mesh.shape["inner"], mesh.shape["outer"]),
        mesh=mesh,
        in_specs=(wide,) * 6 + (P("outer", "inner", None, None),),
        out_specs=(wide,) * 5,
        check_vma=False,
    )
```

```python
import functools

import jax
import jax.numpy as jnp
from jax import lax
from jax.experimental import pallas as pl
from jax.experimental.pallas import tpu as pltpu
from jax.sharding import PartitionSpec as P

D = 128
C = 128
B = 16
BF = jnp.bfloat16
F32 = jnp.float32
MESH = pl.DeviceIdType.MESH
VM = pl.BlockSpec(memory_space=pltpu.VMEM)
DIMS = {"nn": ((1,), (0,)), "nt": ((1,), (1,)), "tn": ((0,), (0,))}


def split(x):
    hi = x.astype(BF)
    return hi, (x - hi.astype(F32)).astype(BF)


def exact(x):
    return x.astype(BF), None


def dot(a, b, mode):
    return lax.dot_general(a, b, (DIMS[mode], ((), ())), preferred_element_type=F32)


def mm(a, b, mode):
    ka = 0 if mode == "tn" else 1
    kb = 1 if mode == "nt" else 0
    (ah, al), (bh, bl) = a, b
    if al is None and bl is None:
        return dot(ah, bh, mode)
    if al is None:
        return dot(jnp.concatenate([ah, ah], ka), jnp.concatenate([bh, bl], kb), mode)
    left = jnp.concatenate([ah, al], ka)
    if bl is None:
        return dot(left, jnp.concatenate([bh, bh], kb), mode)
    top = jnp.concatenate([bh, bl], 1 - kb)
    low = jnp.concatenate([bh, jnp.zeros_like(bl)], 1 - kb)
    both = dot(left, jnp.concatenate([top, low], kb), mode)
    n = both.shape[1] // 2
    return both[:, :n] + both[:, n:]


def iotas():
    return lax.broadcasted_iota(jnp.int32, (C, C), 0), lax.broadcasted_iota(jnp.int32, (C, C), 1)


def ones_where(mask):
    return jnp.where(mask, 1.0, 0.0).astype(BF)


def unit(x):
    r = lax.rsqrt(jnp.sum(x * x, axis=1, keepdims=True) + 1e-06)
    return x * r, r


def decays(gate, row, col):
    wide = gate
    rhs = jnp.concatenate([wide, jnp.where(row > col, wide, 0.0)], 1).astype(BF)
    both = dot(ones_where(row >= col), rhs, "nn")
    after = dot(ones_where(row < col), wide.astype(BF), "nn")
    pair = jnp.where(row >= col, jnp.exp(both[:, C:]), 0.0)
    return jnp.exp(both[:, :C]), jnp.exp(after), pair


def same_block(row, col, size):
    return row // size == col // size


def inverses(lowers, row, col, spread):
    r, lane = row[:B], col[:B]
    packed = []
    for low in lowers:
        parts = [
            jnp.where(lane // B == g, low[g * B : (g + 1) * B], 0.0) for g in range(C // B)
        ]
        while len(parts) > 1:
            parts = [a + b for a, b in zip(parts[::2], parts[1::2])]
        packed.append(parts[0])
    factors = dot(jnp.concatenate(split(jnp.concatenate(packed, 0)), 1), spread[...], "nn")
    small = [jnp.where(lane % B == r, 1.0, 0.0) for _ in lowers]
    for j in range(B - 1):
        small = [
            x - factors[h * B : (h + 1) * B, j * C : (j + 1) * C] * x[j : j + 1]
            for h, x in enumerate(small)
        ]
    done = [
        jnp.concatenate([jnp.where(lane // B == g, x, 0.0) for g in range(C // B)], 0)
        for x in small
    ]
    size = B
    while size < C:
        pick = same_block(row, col, 2 * size) & (row // size != col // size)
        halves = [split(t) for t in done]
        mids = [mm(t, split(jnp.where(pick, low, 0.0)), "nn") for t, low in zip(halves, lowers)]
        done = [t - mm(split(m), h, "nn") for t, m, h in zip(done, mids, halves)]
        size *= 2
    return done


def head_columns(b_ref, g_ref, h):
    heads = b_ref.shape[0]
    pick = ones_where(lax.broadcasted_iota(jnp.int32, (heads, C), 0) == h)
    return jax.nn.sigmoid(dot(b_ref[...], pick, "tn")), dot(g_ref[...], pick, "tn")


def grams(q, k, qr, kr, pair, row, col):
    across = jnp.sum(jnp.where(row == col, kr, 0.0), axis=0, keepdims=True)
    both = dot(jnp.concatenate([q, k], 0), k, "nt")
    scaled = pair * across
    return both[:C] * (qr * scaled), jnp.where(row > col, both[C:] * (kr * scaled), 0.0)


def columns(h):
    return pl.ds(pl.multiple_of(h * D, D), D)


def group_start(hs, args, keep):
    b_ref, g_ref, q_ref, k_ref, _, c_ref = args
    row, col = iotas()
    cols = [head_columns(b_ref, g_ref, h) for h in hs]
    qus = [unit(q_ref[:, columns(h)].astype(F32)) for h in hs]
    qns = [qu[0] for qu in qus]
    krs = [unit(k_ref[:, columns(h)].astype(F32))[1] for h in hs]
    decs = [decays(gate, row, col) for _, gate in cols]
    gms = [
        grams(q_ref[:, columns(h)], k_ref[:, columns(h)], qu[1], kr, d[2], row, col)
        for h, qu, kr, d in zip(hs, qus, krs, decs)
    ]
    cots = [exact(c_ref[:, columns(h)]) for h in hs]
    qparts = [mm(cot, split(qn * d[0]), "tn") for cot, qn, d in zip(cots, qns, decs)]
    pcs = [mm(split(scores), cot, "tn") for (scores, _), cot in zip(gms, cots)]
    for j, h in enumerate(hs):
        for name, value in (
            ("beta", cols[j][0]), ("growth", decs[j][0]), ("tail", decs[j][1]),
            ("pair", decs[j][2]), ("scores", gms[j][0]), ("gram", gms[j][1]),
            ("pc", pcs[j]), ("x", qparts[j]),
        ):
            keep[name][h] = value


def group_solve(hs, keep, spread):
    row, col = iotas()
    lowers = [keep["beta"][h] * keep["gram"][h] for h in hs]
    for h, inv in zip(hs, inverses(lowers, row, col, spread)):
        keep["inv"][h] = inv


def group_end(hs, args, keep, pack, strengths):
    _, _, _, k_ref, v_ref, _ = args
    row, col = iotas()
    eye = row == col
    kns = [unit(k_ref[:, columns(h)].astype(F32))[0] for h in hs]
    grows = [keep["growth"][h] for h in hs]
    invs = [split(keep["inv"][h] * strengths[pl.ds(h, 1), :]) for h in hs]
    wks = [mm(i, split(g * kn), "nn") for i, g, kn in zip(invs, grows, kns)]
    wvs = [mm(i, exact(v_ref[:, columns(h)]), "nn") for i, h in zip(invs, hs)]
    tks = [kn * keep["tail"][h] for kn, h in zip(kns, hs)]
    wss = [split(wk) for wk in wks]
    lasts = [jnp.where(eye, jnp.broadcast_to(g[C - 1 :, :], (C, C)), 0.0) for g in grows]
    lefts = [split(jnp.concatenate([tk, keep["pc"][h]], 1)) for h, tk in zip(hs, tks)]
    outs = [mm(left, ws, "tn") for left, ws in zip(lefts, wss)]
    ms = [last - out[:D] for last, out in zip(lasts, outs)]
    rs = [keep["x"][h] - out[D:] for h, out in zip(hs, outs)]
    ads = [mm((left[0][:, :D], left[1][:, :D]), split(wv), "tn") for left, wv in zip(lefts, wvs)]
    for j, h in enumerate(hs):
        keep["wk"][h] = wks[j]
        keep["wv"][h] = wvs[j]
        pack[0, h, 0] = ms[j]
        pack[0, h, 1] = ads[j]
        pack[0, h, 2] = rs[j]


def state_stage(hs, args, keep, dq_ref):
    _, _, q_ref, k_ref, _, c_ref = args
    qus = [unit(q_ref[:, columns(h)].astype(F32)) for h in hs]
    kns = [unit(k_ref[:, columns(h)].astype(F32))[0] for h in hs]
    cots = [exact(c_ref[:, columns(h)]) for h in hs]
    sss = [split(keep["st"][h]) for h in hs]
    news = [keep["wv"][h] - mm(split(keep["wk"][h]), ss, "nn") for h, ss in zip(hs, sss)]
    dqgs = [keep["growth"][h] * mm(cot, ss, "nt") for h, cot, ss in zip(hs, cots, sss)]
    dscs = [mm(cot, split(new), "nt") for cot, new in zip(cots, news)]
    b1s = [split(dsc * keep["pair"][h]) for h, dsc in zip(hs, dscs)]
    dqns = [mm(b1, split(kn), "nn") + dqg for b1, kn, dqg in zip(b1s, kns, dqgs)]
    wks = [mm(b1, split(qn), "tn") for b1, (qn, _) in zip(b1s, qus)]
    dqs = [
        (qr * (dqn - qn * jnp.sum(dqn * qn, axis=1, keepdims=True))).astype(BF)
        for (qn, qr), dqn in zip(qus, dqns)
    ]
    zs = [dsc * keep["scores"][h] for h, dsc in zip(hs, dscs)]
    for j, h in enumerate(hs):
        dq_ref[:, columns(h)] = dqs[j]
        keep["wv"][h] = news[j]
        keep["wk"][h] = wks[j]
        keep["z"][h] = zs[j]
        keep["x"][h] = dqgs[j] * qus[j][0]


def grad_stage(hs, args, keep, dk_ref, dv_ref, accs):
    _, _, _, k_ref, v_ref, _ = args
    row, col = iotas()
    upper = ones_where(row <= col)
    upper2 = jnp.concatenate([upper, upper], 1)
    lane = lax.broadcasted_iota(jnp.int32, accs[0].shape, 1)
    at = range(len(hs))
    kus = [unit(k_ref[:, columns(h)].astype(F32)) for h in hs]
    betas, grows, tails = ([keep[x][h] for h in hs] for x in ("beta", "growth", "tail"))
    fss = [split(keep["fin"][h]) for h in hs]
    tks = [ku[0] * tail for ku, tail in zip(kus, tails)]
    dnews = [keep["pc"][h] + mm(split(tk), fs, "nt") for h, tk, fs in zip(hs, tks, fss)]
    nss = [split(keep["wv"][h]) for h in hs]
    errs = [mm(split(keep["inv"][h]), split(dnew), "tn") for h, dnew in zip(hs, dnews)]
    dtks = [mm(ns, fs, "nn") for ns, fs in zip(nss, fss)]
    ess = [split(err) for err in errs]
    dlows = [jnp.where(row > col, -mm(es, ns, "nt"), 0.0) for es, ns in zip(ess, nss)]
    dkws = [-mm(es, split(keep["st"][h]), "nt") for es, h in zip(ess, hs)]
    b2s = [dlows[j] * betas[j] * keep["pair"][h] for j, h in enumerate(hs)]
    kss = [split(ku[0]) for ku in kus]
    kgs = [g * d for g, d in zip(grows, dkws)]
    dkns = [
        keep["wk"][h] + mm(split(b2s[j] + b2s[j].T), kss[j], "nn")
        + betas[j] * kgs[j] + tails[j] * dtks[j]
        for j, h in enumerate(hs)
    ]
    dlgs = [dlows[j] * keep["gram"][h] for j, h in enumerate(hs)]
    kgs = [ku[0] * kg for ku, kg in zip(kus, kgs)]
    ups = [
        dot(upper2, jnp.concatenate(split(keep["z"][h] + betas[j] * dlgs[j]), 0), "nn")
        for j, h in enumerate(hs)
    ]
    xs = [
        jnp.sum(keep["x"][h] + betas[j] * kgs[j], axis=1, keepdims=True) for j, h in enumerate(hs)
    ]
    ys = [jnp.sum(dtk * tk, axis=1, keepdims=True) for dtk, tk in zip(dtks, tks)]
    dks = [
        (kr * (dkn - kn * jnp.sum(dkn * kn, axis=1, keepdims=True))).astype(BF)
        for (kn, kr), dkn in zip(kus, dkns)
    ]
    dbetas = [
        jnp.sum(
            (dlgs[j] + kgs[j] + errs[j] * v_ref[:, columns(h)].astype(F32))
            * (betas[j] * (1.0 - betas[j])), axis=1, keepdims=True,
        )
        for j, h in enumerate(hs)
    ]
    totals = [
        jnp.sum(
            jnp.sum(keep["st"][h] * keep["fin"][h].T * grows[j][C - 1 :, :], axis=1, keepdims=True),
            axis=0, keepdims=True,
        )
        for j, h in enumerate(hs)
    ]
    dgates = [
        totals[j] + jnp.sum(
            jnp.where(row > col, ups[j], 0.0), axis=1, keepdims=True,
        )
        for j in at
    ]
    db, dg, xa, ya = (a[...] for a in accs)
    for j, h in enumerate(hs):
        dk_ref[:, columns(h)] = dks[j]
        dv_ref[:, columns(h)] = (betas[j] * errs[j]).astype(BF)
        db, dg = jnp.where(lane == h, dbetas[j], db), jnp.where(lane == h, dgates[j], dg)
        xa, ya = jnp.where(lane == h, xs[j], xa), jnp.where(lane == h, ys[j], ya)
    for acc, value in zip(accs, (db, dg, xa, ya)):
        acc[...] = value


KEPT = (
    "inv", "wk", "wv", "pc", "beta", "growth", "tail",
    "pair", "scores", "gram", "z", "x", "st", "fin",
)
OWN = ("sin", "sout", "sgive", "dz", "dp", "eout", "fgive", "vout")
TWICE = ("aup", "xout", "pin")
SENDS = ("state", "pack", "up", "mid", "down", "pair", "near", "far", "relay", "fin")
RECVS = ("state", "pack", "mid", "down", "pair", "far", "relay", "fin")
QUAD, DUO = 4, 2
STEPS = 3
HOP_UP, HOP, HOP_OUT, HOP_BACK = 3, 3, 2, 4
LATE_UP = 2
CLOSE = 2


def pair_of(ref, k):
    return ref[k, :, :D], ref[k, :, D:]


def chain_kernel(
    heads, n, n_outer,
    b_ref, g_ref, q_ref, k_ref, v_ref, c_ref, s0_ref,
    dq_ref, dk_ref, dv_ref, db_ref, dg_ref,
    *scratch,
):
    args = (b_ref, g_ref, q_ref, k_ref, v_ref, c_ref)
    scratch = list(scratch)
    keep = {x: scratch.pop(0) for x in KEPT}
    sin, sout, sgive, dz, dp, eout, fgive, vout = (scratch.pop(0) for _ in OWN)
    aup, xout, pin = (scratch.pop(0) for _ in TWICE)
    pack, duo, both, spread, strengths = (scratch.pop(0) for _ in range(5))
    accs = [scratch.pop(0) for _ in range(4)]
    send = {x: scratch.pop(0) for x in SENDS}
    recv = {x: scratch.pop(0) for x in RECVS}
    st, fin = keep["st"], keep["fin"]
    o, i = lax.axis_index("outer"), lax.axis_index("inner")
    z, c = i // 2, lax.rem(i, 2)
    chips, own, quads = n // 2, heads // 2, heads // QUAD
    hpd = s0_ref.shape[0]
    top = z == chips - 1
    zz = jnp.where(c == 0, z, chips - 1 - z)
    root, leaf = zz == 0, zz == chips - 1
    final_block = o == n_outer - 1
    even = lax.rem(o, 2) == 0
    barrier = pltpu.get_barrier_semaphore()
    for d in range(1, n):
        pl.semaphore_signal(
            barrier, inc=1, device_id=(o, lax.rem(i + d, n)), device_id_type=MESH
        )
    for d in range(1, n_outer):
        pl.semaphore_signal(
            barrier, inc=1, device_id=(lax.rem(o + d, n_outer), i), device_id_type=MESH
        )

    def remote(src, dst, give, take, k, target):
        return pltpu.make_async_remote_copy(
            src_ref=src, dst_ref=dst, send_sem=send[give], recv_sem=recv[take].at[k],
            device_id=target, device_id_type=MESH,
        )

    mate = (o, i + 1 - 2 * c)
    above = (o, lax.rem(i + 2, n))
    inward = (o, lax.rem(i + n - 2 + 4 * c, n))
    outward = (o, lax.rem(i + n + 2 - 4 * c, n))
    before = (lax.rem(o + n_outer - 1, n_outer), i)
    before2 = (lax.rem(o + n_outer - 2, n_outer), i)

    def pack_copy(k):
        h = 2 * k + 1 - c
        return remote(pack.at[0, h], pack.at[1, h], "pack", "pack", k, mate)

    def up_copy(k):
        return remote(sout.at[k], sin.at[k], "up", "state", k, above)

    def mid_copy(k):
        return remote(sgive.at[k], st.at[2 * k + c], "mid", "mid", k, mate)

    def down_copy(k):
        return remote(xout.at[k], duo.at[0, k], "down", "down", k, inward)

    def pair_copy(k):
        return remote(xout.at[k], pin.at[k], "pair", "pair", k, before)

    def near_copy(k):
        return remote(eout.at[k], dz.at[k], "near", "relay", k, before)

    def far_copy(k):
        return remote(eout.at[k], dp.at[k], "far", "far", k, before2)

    def relay_copy(k):
        return remote(dz.at[k], dz.at[k], "relay", "relay", k, outward)

    def pass_copy(k):
        return remote(vout.at[k], dz.at[k], "relay", "relay", k, outward)

    def fin_copy(k):
        return remote(fgive.at[k], fin.at[2 * k + c], "fin", "fin", k, mate)

    for j in range(hpd):
        h = i * hpd + j

        @pl.when(i == lax.rem(h, 2))
        def _():
            k = h // 2
            pltpu.make_async_copy(s0_ref.at[j], sin.at[k], recv["state"].at[k]).start()

    def begin():
        pl.semaphore_wait(barrier, n + n_outer - 2)
        for j in range(hpd):
            h = i * hpd + j
            owner = lax.rem(h, 2)

            @pl.when(i != owner)
            def _():
                pltpu.make_async_remote_copy(
                    src_ref=s0_ref.at[j], dst_ref=sin.at[h // 2], send_sem=send["state"],
                    recv_sem=recv["state"].at[h // 2], device_id=(o, owner), device_id_type=MESH,
                ).start()

    row, col = iotas()
    for j in range(B - 1):
        ones = ones_where(same_block(row, col, B) & (row % B == j))
        spread[:, j * C : (j + 1) * C] = jnp.concatenate([ones, ones], 0)
    strengths[...] = jax.nn.sigmoid(b_ref[...].astype(F32))
    for acc in accs:
        acc[...] = jnp.zeros_like(acc)

    @pl.when(final_block & ((c == 0) | root))
    def _():
        dz[...] = jnp.zeros_like(dz)

    @pl.when((o == n_outer - 2) & root)
    def _():
        dp[...] = jnp.zeros_like(dp)

    @pl.when(leaf)
    def _():
        row, col = iotas()
        ident = jnp.where(row == col, 1.0, 0.0)
        for k in range(own):
            duo[0, k] = jnp.concatenate([jnp.zeros_like(ident), ident], 0)

    relays = jnp.logical_not(leaf) & (jnp.logical_not(final_block) | (c == 1))
    landing = jnp.where(root, jnp.logical_not(even | final_block), jnp.logical_not(final_block) | (c == 1))
    lag_down = HOP * (chips - 1 - zz)
    lag_root = HOP * (chips - 1) + HOP_OUT * (n_outer // 2 - o // 2)
    ends = [
        jnp.where(final_block, HOP * (chips - 1 - z), lag_root + HOP_BACK * z),
        jnp.where(final_block, 0, lag_root) + HOP_BACK * (chips - 1 - z),
    ]
    lag_up = LATE_UP + HOP_UP * z

    def third(x):
        return (x * 43) >> 7

    def start_of(k):
        return STEPS * (k >> 1) + (k & 1) + STEPS

    def at(t, lag):
        late = t - lag - STEPS
        whole = third(late)
        part = late - STEPS * whole
        k = 2 * whole + part
        ok = (late >= 0) & (part < 2) & (k < own)
        return ok, k

    heavy = STEPS * quads
    last_start = STEPS * ((own - 1) // 2) + (own - 1) % 2 + STEPS
    state_base = jnp.maximum(heavy, last_start + lag_up + 1 - (own - 1))
    def end_ticks(lag, depth):
        found = []
        for k in range(own):
            due = start_of(k) + lag - ((k * depth) >> CLOSE)
            found.append(jnp.maximum(due, found[-1] + 1) if k else due)
        return found

    both_ends = [
        end_ticks(ends[0], jnp.where(final_block, 0, z)), end_ticks(ends[1], chips - 1 - z)
    ]
    my_ends = [jnp.where(c == 0, x, y) for x, y in zip(*both_ends)]
    grad_ticks = []
    for j, (x, y) in enumerate(zip(*both_ends)):
        due = jnp.maximum(jnp.maximum(x, y) + 1, state_base + own + j)
        grad_ticks.append(jnp.maximum(due, grad_ticks[-1] + 1) if j else due)
    ticks = grad_ticks[-1] + 1

    def listed(t, table):
        k, hit = jnp.int32(0), False
        for when in table:
            k += (when < t).astype(jnp.int32)
            hit = hit | (when == t)
        return hit, k

    def combine(k):
        h = 2 * k + c

        def part(slot):
            return pack[slot, h, 0], pack[slot, h, 1], pack[slot, h, 2]

        me, ae, re = part(c)
        mo, ao, ro = part(1 - c)
        mes = split(me)
        both_rows = mm(split(jnp.concatenate([mo, ro], 0)), mes, "nn")
        joined = both_rows[:D]
        back = both_rows[D:] + re
        aoe = mm(split(mo), split(ae), "nn") + ao
        both[k] = jnp.concatenate(
            [jnp.concatenate(split(joined), 1), jnp.concatenate(mes, 1)], 0
        )
        aup[k] = jnp.concatenate([aoe, ae], 0)
        whole = jnp.concatenate([back, joined], 0)
        duo[1, k] = whole

        @pl.when(leaf)
        def _():
            xout[k] = whole

    def tick(t, carry):
        q = third(t)
        step = t - STEPS * q
        in_group = t < heavy

        @pl.when(in_group & (step == 0))
        def _():
            group_start([q * QUAD + s for s in range(QUAD)], args, keep)

        @pl.when(in_group & (step == 1))
        def _():
            group_solve([q * QUAD + s for s in range(QUAD)], keep, spread)

        @pl.when(in_group & (step == 2))
        def _():
            group_end([q * QUAD + s for s in range(QUAD)], args, keep, pack, strengths)

            @pl.when(t == STEPS - 1)
            def _():
                begin()

            for s in range(2):
                pack_copy(2 * q + s).start()

        j = t - state_base

        @pl.when((j >= 0) & (j < own))
        def _():
            mid_copy(j).wait_recv()
            state_stage([2 * j, 2 * j + 1], args, keep, dq_ref)

        hit, j = listed(t, grad_ticks)

        @pl.when(hit)
        def _():
            fin_copy(j).wait_recv()
            grad_stage([2 * j, 2 * j + 1], args, keep, dk_ref, dv_ref, accs)

        ok, kc = at(t, 0)

        @pl.when(ok)
        def _():
            pack_copy(kc).wait_recv()
            combine(kc)

            @pl.when(leaf)
            def _():
                down_copy(kc).start()

        up_ok, ku = at(t, lag_up)
        down_ok, kd = at(t, lag_down)
        down_ok = down_ok & jnp.logical_not(leaf)

        @pl.when(down_ok)
        def _():
            down_copy(kd).wait_recv()
            near = duo[1 - c, kd]
            back = mm(split(duo[c, kd]), split(near[D:]), "nn")
            xout[kd] = jnp.concatenate([back[:D] + near[:D], back[D:]], 0)

            @pl.when(jnp.logical_not(root))
            def _():
                down_copy(kd).start()

            @pl.when(root & jnp.logical_not(even))
            def _():
                pair_copy(kd).start()

        @pl.when(up_ok)
        def _():
            pltpu.make_async_copy(sin.at[ku], sin.at[ku], recv["state"].at[ku]).wait()
            state = sin[ku]
            moved = mm(pair_of(both, ku), split(state), "nn") + aup[ku]
            sout[ku] = moved[:D]
            mid = moved[D:]
            st[2 * ku + c] = jnp.where(c == 0, state, mid)
            sgive[ku] = jnp.where(c == 0, mid, state)

            @pl.when(jnp.logical_not(top))
            def _():
                up_copy(ku).start()

            mid_copy(ku).start()

        d_ok, k = listed(t, my_ends)

        @pl.when(d_ok & root & even)
        def _():
            pair_copy(k).wait_recv()

            @pl.when(o < n_outer - 2)
            def _():
                far_copy(k).wait_recv()

            end = pin[k, :D, :] + mm(split(dp[k]), split(pin[k, D:, :]), "nn")
            dz[k] = end

            @pl.when(o > 0)
            def _():
                eout[k] = xout[k, :D, :] + mm(split(end), split(xout[k, D:, :]), "nn")
                near_copy(k).start()
                far_copy(k).start()

        @pl.when(d_ok & landing)
        def _():
            relay_copy(k).wait_recv()

        @pl.when(d_ok & relays & (c == 0))
        def _():
            relay_copy(k).start()

        @pl.when(d_ok)
        def _():
            h = 2 * k + c
            end = dz[k]
            value = duo[c, k, :D, :] + mm(split(end), split(duo[c, k, D:, :]), "nn")

            @pl.when(relays & (c == 1))
            def _():
                vout[k] = value
                pass_copy(k).start()

            odd_end = jnp.where(c == 0, value, end)
            even_end = pack[1 - c, h, 2] + mm(split(odd_end), split(pack[1 - c, h, 0]), "nn")
            fin[h] = jnp.where(c == 0, even_end, odd_end)
            fgive[k] = jnp.where(c == 0, odd_end, even_end)
            fin_copy(k).start()

        return carry

    lax.fori_loop(0, ticks, tick, 0)
    db, dg, xa, ya = (acc[...] for acc in accs)
    sums = jnp.concatenate([*split(xa), *split(ya)], 0)
    upper, lower = ones_where(row <= col), ones_where(row > col)
    dg = dg + dot(jnp.concatenate([upper, upper, lower, lower], 1), sums, "nn")
    db_ref[...] = db.T[:heads].astype(BF)
    dg_ref[...] = dg.T[:heads].astype(BF)

    for j in range(hpd):
        h = i * hpd + j
        owner = lax.rem(h, 2)

        @pl.when(i != owner)
        def _():
            pltpu.make_async_remote_copy(
                src_ref=s0_ref.at[j], dst_ref=sin.at[h // 2], send_sem=send["state"],
                recv_sem=recv["state"].at[h // 2], device_id=(o, owner), device_id_type=MESH,
            ).wait_send()

    def sent(kind, ref):
        every = ref.at[pl.ds(0, own)]
        pltpu.make_async_copy(every, every, send[kind]).wait()

    sent("pack", pack.at[0])
    sent("mid", sgive)
    sent("fin", fgive)

    @pl.when(jnp.logical_not(top))
    def _():
        sent("up", sout)

    @pl.when(jnp.logical_not(root))
    def _():
        sent("down", xout)

    @pl.when(root & jnp.logical_not(even))
    def _():
        sent("pair", xout)

    @pl.when(root & even & (o > 0))
    def _():
        sent("near", eout)
        sent("far", eout)

    @pl.when(relays)
    def _():
        sent("relay", dz)


def shards(n, n_outer, queries, key_rows, value_rows, beta_logit, log_gate, out_grad, block_states):
    heads = beta_logit.shape[1]
    own = heads // 2
    big = jax.ShapeDtypeStruct(queries.shape, BF)
    thin = jax.ShapeDtypeStruct((heads, C), BF)
    acc = pltpu.VMEM((C, D), F32)
    sems = pltpu.SemaphoreType.DMA((own,))
    dq, dk, dv, db, dg = pl.pallas_call(
        functools.partial(chain_kernel, heads, n, n_outer),
        out_shape=tuple(pltpu.VMEM(x.shape, x.dtype) for x in (big, big, big, thin, thin)),
        in_specs=[VM] * 7,
        out_specs=(VM,) * 5,
        scratch_shapes=[pltpu.VMEM((heads + 2, D, D), F32)] * len(KEPT)
        + [pltpu.VMEM((own + 1, D, D), F32)] * len(OWN)
        + [pltpu.VMEM((own + 1, 2 * D, D), F32)] * len(TWICE)
        + [
            pltpu.VMEM((2, heads, 3, D, D), F32),
            pltpu.VMEM((2, own + 1, 2 * D, D), F32),
            pltpu.VMEM((own + 1, 2 * D, 2 * D), BF),
            pltpu.VMEM((2 * C, (B - 1) * C), BF),
            pltpu.VMEM((heads, C), F32),
            acc, acc, acc, acc,
        ]
        + [pltpu.SemaphoreType.DMA] * len(SENDS) + [sems] * len(RECVS),
        compiler_params=pltpu.CompilerParams(
            vmem_limit_bytes=56 << 20, collective_id=0, has_side_effects=True
        ),
    )(beta_logit.T, log_gate.T, queries, key_rows, value_rows, out_grad, block_states[0])

    def hand_on(*refs):
        sem = refs[10]
        copies = [
            pltpu.make_async_copy(src, dst, sem.at[j])
            for j, (src, dst) in enumerate(zip(refs[:5], refs[5:10]))
        ]
        for copy in copies:
            copy.start()
        for copy in copies:
            copy.wait()

    dq, dk, dv, db, dg = pl.pallas_call(
        hand_on, out_shape=(big, big, big, thin, thin), in_specs=[VM] * 5,
        out_specs=(pl.BlockSpec(memory_space=pl.ANY),) * 5,
        scratch_shapes=[pltpu.SemaphoreType.DMA((5,))],
    )(*(pltpu.with_memory_space_constraint(x, pltpu.VMEM) for x in (dq, dk, dv, db, dg)))
    return dq, dk, dv, db.T, dg.T


def solution(mesh):
    wide = P(("outer", "inner"), None)
    return jax.shard_map(
        functools.partial(shards, mesh.shape["inner"], mesh.shape["outer"]),
        mesh=mesh,
        in_specs=(wide,) * 6 + (P("outer", "inner", None, None),),
        out_specs=(wide,) * 5,
        check_vma=False,
    )
```

```python
import functools

import jax
import jax.numpy as jnp
from jax import lax
from jax.experimental import pallas as pl
from jax.experimental.pallas import tpu as pltpu
from jax.sharding import PartitionSpec as P

D = 128
C = 128
B = 16
BF = jnp.bfloat16
F32 = jnp.float32
MESH = pl.DeviceIdType.MESH
VM = pl.BlockSpec(memory_space=pltpu.VMEM)
DIMS = {"nn": ((1,), (0,)), "nt": ((1,), (1,)), "tn": ((0,), (0,))}


def split(x):
    hi = x.astype(BF)
    return hi, (x - hi.astype(F32)).astype(BF)


def exact(x):
    return x.astype(BF), None


def dot(a, b, mode):
    return lax.dot_general(a, b, (DIMS[mode], ((), ())), preferred_element_type=F32)


def mm(a, b, mode):
    ka = 0 if mode == "tn" else 1
    kb = 1 if mode == "nt" else 0
    (ah, al), (bh, bl) = a, b
    if al is None and bl is None:
        return dot(ah, bh, mode)
    if al is None:
        return dot(jnp.concatenate([ah, ah], ka), jnp.concatenate([bh, bl], kb), mode)
    left = jnp.concatenate([ah, al], ka)
    if bl is None:
        return dot(left, jnp.concatenate([bh, bh], kb), mode)
    top = jnp.concatenate([bh, bl], 1 - kb)
    low = jnp.concatenate([bh, jnp.zeros_like(bl)], 1 - kb)
    both = dot(left, jnp.concatenate([top, low], kb), mode)
    n = both.shape[1] // 2
    return both[:, :n] + both[:, n:]


def iotas():
    return lax.broadcasted_iota(jnp.int32, (C, C), 0), lax.broadcasted_iota(jnp.int32, (C, C), 1)


def ones_where(mask):
    return jnp.where(mask, 1.0, 0.0).astype(BF)


def unit(x):
    r = lax.rsqrt(jnp.sum(x * x, axis=1, keepdims=True) + 1e-06)
    return x * r, r


def decays(gate, row, col):
    wide = gate
    rhs = jnp.concatenate([wide, jnp.where(row > col, wide, 0.0)], 1).astype(BF)
    both = dot(ones_where(row >= col), rhs, "nn")
    after = dot(ones_where(row < col), wide.astype(BF), "nn")
    pair = jnp.where(row >= col, jnp.exp(both[:, C:]), 0.0)
    return jnp.exp(both[:, :C]), jnp.exp(after), pair


def same_block(row, col, size):
    return row // size == col // size


def inverses(lowers, row, col, spread):
    r, lane = row[:B], col[:B]
    packed = []
    for low in lowers:
        parts = [
            jnp.where(lane // B == g, low[g * B : (g + 1) * B], 0.0) for g in range(C // B)
        ]
        while len(parts) > 1:
            parts = [a + b for a, b in zip(parts[::2], parts[1::2])]
        packed.append(parts[0])
    factors = dot(jnp.concatenate(split(jnp.concatenate(packed, 0)), 1), spread[...], "nn")
    small = [jnp.where(lane % B == r, 1.0, 0.0) for _ in lowers]
    for j in range(B - 1):
        small = [
            x - factors[h * B : (h + 1) * B, j * C : (j + 1) * C] * x[j : j + 1]
            for h, x in enumerate(small)
        ]
    done = [
        jnp.concatenate([jnp.where(lane // B == g, x, 0.0) for g in range(C // B)], 0)
        for x in small
    ]
    size = B
    while size < C:
        pick = same_block(row, col, 2 * size) & (row // size != col // size)
        halves = [split(t) for t in done]
        mids = [mm(t, split(jnp.where(pick, low, 0.0)), "nn") for t, low in zip(halves, lowers)]
        done = [t - mm(split(m), h, "nn") for t, m, h in zip(done, mids, halves)]
        size *= 2
    return done


def head_columns(b_ref, g_ref, h):
    heads = b_ref.shape[0]
    pick = ones_where(lax.broadcasted_iota(jnp.int32, (heads, C), 0) == h)
    return jax.nn.sigmoid(dot(b_ref[...], pick, "tn")), dot(g_ref[...], pick, "tn")


def grams(q, k, qr, kr, pair, row, col):
    across = jnp.sum(jnp.where(row == col, kr, 0.0), axis=0, keepdims=True)
    both = dot(jnp.concatenate([q, k], 0), k, "nt")
    scaled = pair * across
    return both[:C] * (qr * scaled), jnp.where(row > col, both[C:] * (kr * scaled), 0.0)


def columns(h):
    return pl.ds(pl.multiple_of(h * D, D), D)


def group_start(hs, args, keep):
    b_ref, g_ref, q_ref, k_ref, _, c_ref = args
    row, col = iotas()
    cols = [head_columns(b_ref, g_ref, h) for h in hs]
    qus = [unit(q_ref[:, columns(h)].astype(F32)) for h in hs]
    qns = [qu[0] for qu in qus]
    krs = [unit(k_ref[:, columns(h)].astype(F32))[1] for h in hs]
    decs = [decays(gate, row, col) for _, gate in cols]
    gms = [
        grams(q_ref[:, columns(h)], k_ref[:, columns(h)], qu[1], kr, d[2], row, col)
        for h, qu, kr, d in zip(hs, qus, krs, decs)
    ]
    cots = [exact(c_ref[:, columns(h)]) for h in hs]
    qparts = [mm(cot, split(qn * d[0]), "tn") for cot, qn, d in zip(cots, qns, decs)]
    pcs = [mm(split(scores), cot, "tn") for (scores, _), cot in zip(gms, cots)]
    for j, h in enumerate(hs):
        for name, value in (
            ("beta", cols[j][0]), ("growth", decs[j][0]), ("tail", decs[j][1]),
            ("pair", decs[j][2]), ("scores", gms[j][0]), ("gram", gms[j][1]),
            ("pc", pcs[j]), ("x", qparts[j]),
        ):
            keep[name][h] = value


def group_solve(hs, keep, spread):
    row, col = iotas()
    lowers = [keep["beta"][h] * keep["gram"][h] for h in hs]
    for h, inv in zip(hs, inverses(lowers, row, col, spread)):
        keep["inv"][h] = inv


def group_end(hs, args, keep, pack, strengths):
    _, _, _, k_ref, v_ref, _ = args
    row, col = iotas()
    eye = row == col
    kns = [unit(k_ref[:, columns(h)].astype(F32))[0] for h in hs]
    grows = [keep["growth"][h] for h in hs]
    invs = [split(keep["inv"][h] * strengths[pl.ds(h, 1), :]) for h in hs]
    wks = [mm(i, split(g * kn), "nn") for i, g, kn in zip(invs, grows, kns)]
    wvs = [mm(i, exact(v_ref[:, columns(h)]), "nn") for i, h in zip(invs, hs)]
    tks = [kn * keep["tail"][h] for kn, h in zip(kns, hs)]
    wss = [split(wk) for wk in wks]
    lasts = [jnp.where(eye, jnp.broadcast_to(g[C - 1 :, :], (C, C)), 0.0) for g in grows]
    lefts = [split(jnp.concatenate([tk, keep["pc"][h]], 1)) for h, tk in zip(hs, tks)]
    outs = [mm(left, ws, "tn") for left, ws in zip(lefts, wss)]
    ms = [last - out[:D] for last, out in zip(lasts, outs)]
    rs = [keep["x"][h] - out[D:] for h, out in zip(hs, outs)]
    ads = [mm((left[0][:, :D], left[1][:, :D]), split(wv), "tn") for left, wv in zip(lefts, wvs)]
    for j, h in enumerate(hs):
        keep["wk"][h] = wks[j]
        keep["wv"][h] = wvs[j]
        pack[0, h, 0] = ms[j]
        pack[0, h, 1] = ads[j]
        pack[0, h, 2] = rs[j]


def state_stage(hs, args, keep, dq_ref):
    _, _, q_ref, k_ref, _, c_ref = args
    qus = [unit(q_ref[:, columns(h)].astype(F32)) for h in hs]
    kns = [unit(k_ref[:, columns(h)].astype(F32))[0] for h in hs]
    cots = [exact(c_ref[:, columns(h)]) for h in hs]
    sss = [split(keep["st"][h]) for h in hs]
    news = [keep["wv"][h] - mm(split(keep["wk"][h]), ss, "nn") for h, ss in zip(hs, sss)]
    dqgs = [keep["growth"][h] * mm(cot, ss, "nt") for h, cot, ss in zip(hs, cots, sss)]
    dscs = [mm(cot, split(new), "nt") for cot, new in zip(cots, news)]
    b1s = [split(dsc * keep["pair"][h]) for h, dsc in zip(hs, dscs)]
    dqns = [mm(b1, split(kn), "nn") + dqg for b1, kn, dqg in zip(b1s, kns, dqgs)]
    wks = [mm(b1, split(qn), "tn") for b1, (qn, _) in zip(b1s, qus)]
    dqs = [
        (qr * (dqn - qn * jnp.sum(dqn * qn, axis=1, keepdims=True))).astype(BF)
        for (qn, qr), dqn in zip(qus, dqns)
    ]
    zs = [dsc * keep["scores"][h] for h, dsc in zip(hs, dscs)]
    for j, h in enumerate(hs):
        dq_ref[:, columns(h)] = dqs[j]
        keep["wv"][h] = news[j]
        keep["wk"][h] = wks[j]
        keep["z"][h] = zs[j]
        keep["x"][h] = dqgs[j] * qus[j][0]


def grad_stage(hs, args, keep, dk_ref, dv_ref, accs):
    _, _, _, k_ref, v_ref, _ = args
    row, col = iotas()
    upper = ones_where(row <= col)
    upper2 = jnp.concatenate([upper, upper], 1)
    lane = lax.broadcasted_iota(jnp.int32, accs[0].shape, 1)
    at = range(len(hs))
    kus = [unit(k_ref[:, columns(h)].astype(F32)) for h in hs]
    betas, grows, tails = ([keep[x][h] for h in hs] for x in ("beta", "growth", "tail"))
    fss = [split(keep["fin"][h]) for h in hs]
    tks = [ku[0] * tail for ku, tail in zip(kus, tails)]
    dnews = [keep["pc"][h] + mm(split(tk), fs, "nt") for h, tk, fs in zip(hs, tks, fss)]
    nss = [split(keep["wv"][h]) for h in hs]
    errs = [mm(split(keep["inv"][h]), split(dnew), "tn") for h, dnew in zip(hs, dnews)]
    dtks = [mm(ns, fs, "nn") for ns, fs in zip(nss, fss)]
    ess = [split(err) for err in errs]
    dlows = [jnp.where(row > col, -mm(es, ns, "nt"), 0.0) for es, ns in zip(ess, nss)]
    dkws = [-mm(es, split(keep["st"][h]), "nt") for es, h in zip(ess, hs)]
    b2s = [dlows[j] * betas[j] * keep["pair"][h] for j, h in enumerate(hs)]
    kss = [split(ku[0]) for ku in kus]
    kgs = [g * d for g, d in zip(grows, dkws)]
    dkns = [
        keep["wk"][h] + mm(split(b2s[j] + b2s[j].T), kss[j], "nn")
        + betas[j] * kgs[j] + tails[j] * dtks[j]
        for j, h in enumerate(hs)
    ]
    dlgs = [dlows[j] * keep["gram"][h] for j, h in enumerate(hs)]
    kgs = [ku[0] * kg for ku, kg in zip(kus, kgs)]
    ups = [
        dot(upper2, jnp.concatenate(split(keep["z"][h] + betas[j] * dlgs[j]), 0), "nn")
        for j, h in enumerate(hs)
    ]
    xs = [
        jnp.sum(keep["x"][h] + betas[j] * kgs[j], axis=1, keepdims=True) for j, h in enumerate(hs)
    ]
    ys = [jnp.sum(dtk * tk, axis=1, keepdims=True) for dtk, tk in zip(dtks, tks)]
    dks = [
        (kr * (dkn - kn * jnp.sum(dkn * kn, axis=1, keepdims=True))).astype(BF)
        for (kn, kr), dkn in zip(kus, dkns)
    ]
    dbetas = [
        jnp.sum(
            (dlgs[j] + kgs[j] + errs[j] * v_ref[:, columns(h)].astype(F32))
            * (betas[j] * (1.0 - betas[j])), axis=1, keepdims=True,
        )
        for j, h in enumerate(hs)
    ]
    totals = [
        jnp.sum(
            jnp.sum(keep["st"][h] * keep["fin"][h].T * grows[j][C - 1 :, :], axis=1, keepdims=True),
            axis=0, keepdims=True,
        )
        for j, h in enumerate(hs)
    ]
    dgates = [
        totals[j] + jnp.sum(
            jnp.where(row > col, ups[j], 0.0), axis=1, keepdims=True,
        )
        for j in at
    ]
    db, dg, xa, ya = (a[...] for a in accs)
    for j, h in enumerate(hs):
        dk_ref[:, columns(h)] = dks[j]
        dv_ref[:, columns(h)] = (betas[j] * errs[j]).astype(BF)
        db, dg = jnp.where(lane == h, dbetas[j], db), jnp.where(lane == h, dgates[j], dg)
        xa, ya = jnp.where(lane == h, xs[j], xa), jnp.where(lane == h, ys[j], ya)
    for acc, value in zip(accs, (db, dg, xa, ya)):
        acc[...] = value


KEPT = (
    "inv", "wk", "wv", "pc", "beta", "growth", "tail",
    "pair", "scores", "gram", "z", "x", "st", "fin",
)
OWN = ("sin", "sout", "sgive", "dz", "dp", "eout", "fgive", "vout")
TWICE = ("aup", "xout", "pin")
SENDS = ("state", "pack", "up", "mid", "down", "pair", "near", "far", "relay", "fin")
RECVS = ("state", "pack", "mid", "down", "pair", "far", "relay", "fin")
QUAD, DUO = 4, 2
STEPS = 3
HOP_UP, HOP, HOP_OUT, HOP_BACK = 3, 3, 2, 4
LATE_UP = 2
CLOSE = 2


def pair_of(ref, k):
    return ref[k, :, :D], ref[k, :, D:]


def chain_kernel(
    heads, n, n_outer,
    b_ref, g_ref, q_ref, k_ref, v_ref, c_ref, s0_ref,
    dq_ref, dk_ref, dv_ref, db_ref, dg_ref,
    *scratch,
):
    args = (b_ref, g_ref, q_ref, k_ref, v_ref, c_ref)
    scratch = list(scratch)
    keep = {x: scratch.pop(0) for x in KEPT}
    sin, sout, sgive, dz, dp, eout, fgive, vout = (scratch.pop(0) for _ in OWN)
    aup, xout, pin = (scratch.pop(0) for _ in TWICE)
    pack, duo, both, spread, strengths = (scratch.pop(0) for _ in range(5))
    accs = [scratch.pop(0) for _ in range(4)]
    send = {x: scratch.pop(0) for x in SENDS}
    recv = {x: scratch.pop(0) for x in RECVS}
    st, fin = keep["st"], keep["fin"]
    o, i = lax.axis_index("outer"), lax.axis_index("inner")
    z, c = i // 2, lax.rem(i, 2)
    chips, own, quads = n // 2, heads // 2, heads // QUAD
    hpd = s0_ref.shape[0]
    top = z == chips - 1
    zz = jnp.where(c == 0, z, chips - 1 - z)
    root, leaf = zz == 0, zz == chips - 1
    chained = (o > 0) | (c == 0)
    final_block = o == n_outer - 1
    even = lax.rem(o, 2) == 0
    barrier = pltpu.get_barrier_semaphore()
    for d in range(1, n):
        pl.semaphore_signal(
            barrier, inc=1, device_id=(o, lax.rem(i + d, n)), device_id_type=MESH
        )
    for d in range(1, n_outer):
        pl.semaphore_signal(
            barrier, inc=1, device_id=(lax.rem(o + d, n_outer), i), device_id_type=MESH
        )

    def remote(src, dst, give, take, k, target):
        return pltpu.make_async_remote_copy(
            src_ref=src, dst_ref=dst, send_sem=send[give], recv_sem=recv[take].at[k],
            device_id=target, device_id_type=MESH,
        )

    mate = (o, i + 1 - 2 * c)
    above = (o, lax.rem(i + 2, n))
    inward = (o, lax.rem(i + n - 2 + 4 * c, n))
    outward = (o, lax.rem(i + n + 2 - 4 * c, n))
    before = (lax.rem(o + n_outer - 1, n_outer), i)
    before2 = (lax.rem(o + n_outer - 2, n_outer), i)

    def pack_copy(k):
        h = 2 * k + 1 - c
        return remote(pack.at[0, h], pack.at[1, h], "pack", "pack", k, mate)

    def up_copy(k):
        return remote(sout.at[k], sin.at[k], "up", "state", k, above)

    def mid_copy(k):
        return remote(sgive.at[k], st.at[2 * k + c], "mid", "mid", k, mate)

    def down_copy(k):
        return remote(xout.at[k], duo.at[0, k], "down", "down", k, inward)

    def pair_copy(k):
        return remote(xout.at[k], pin.at[k], "pair", "pair", k, before)

    def near_copy(k):
        return remote(eout.at[k], dz.at[k], "near", "relay", k, before)

    def far_copy(k):
        return remote(eout.at[k], dp.at[k], "far", "far", k, before2)

    def relay_copy(k):
        return remote(dz.at[k], dz.at[k], "relay", "relay", k, outward)

    def pass_copy(k):
        return remote(vout.at[k], dz.at[k], "relay", "relay", k, outward)

    def fin_copy(k):
        return remote(fgive.at[k], fin.at[2 * k + c], "fin", "fin", k, mate)

    for j in range(hpd):
        h = i * hpd + j

        @pl.when(i == lax.rem(h, 2))
        def _():
            k = h // 2
            pltpu.make_async_copy(s0_ref.at[j], sin.at[k], recv["state"].at[k]).start()

    def begin():
        pl.semaphore_wait(barrier, n + n_outer - 2)
        for j in range(hpd):
            h = i * hpd + j
            owner = lax.rem(h, 2)

            @pl.when(i != owner)
            def _():
                pltpu.make_async_remote_copy(
                    src_ref=s0_ref.at[j], dst_ref=sin.at[h // 2], send_sem=send["state"],
                    recv_sem=recv["state"].at[h // 2], device_id=(o, owner), device_id_type=MESH,
                ).start()

    row, col = iotas()
    for j in range(B - 1):
        ones = ones_where(same_block(row, col, B) & (row % B == j))
        spread[:, j * C : (j + 1) * C] = jnp.concatenate([ones, ones], 0)
    strengths[...] = jax.nn.sigmoid(b_ref[...].astype(F32))
    for acc in accs:
        acc[...] = jnp.zeros_like(acc)

    @pl.when(final_block & ((c == 0) | root))
    def _():
        dz[...] = jnp.zeros_like(dz)

    @pl.when((o == n_outer - 2) & root)
    def _():
        dp[...] = jnp.zeros_like(dp)

    @pl.when(leaf)
    def _():
        row, col = iotas()
        ident = jnp.where(row == col, 1.0, 0.0)
        for k in range(own):
            duo[0, k] = jnp.concatenate([jnp.zeros_like(ident), ident], 0)

    relays = jnp.logical_not(leaf) & (jnp.logical_not(final_block) | (c == 1))
    landing = jnp.where(root, jnp.logical_not(even | final_block), jnp.logical_not(final_block) | (c == 1))
    lag_down = HOP * (chips - 1 - zz)
    lag_root = HOP * (chips - 1) + HOP_OUT * (n_outer // 2 - o // 2)
    ends = [
        jnp.where(final_block, HOP * (chips - 1 - z), lag_root + HOP_BACK * z),
        jnp.where(final_block, 0, lag_root) + HOP_BACK * (chips - 1 - z),
    ]
    lag_up = LATE_UP + HOP_UP * z

    def third(x):
        return (x * 43) >> 7

    def start_of(k):
        return STEPS * (k >> 1) + (k & 1) + STEPS

    def at(t, lag):
        late = t - lag - STEPS
        whole = third(late)
        part = late - STEPS * whole
        k = 2 * whole + part
        ok = (late >= 0) & (part < 2) & (k < own)
        return ok, k

    heavy = STEPS * quads
    last_start = STEPS * ((own - 1) // 2) + (own - 1) % 2 + STEPS
    state_base = jnp.maximum(heavy, last_start + lag_up + 1 - (own - 1))
    def end_ticks(lag, depth):
        found = []
        for k in range(own):
            due = start_of(k) + lag - ((k * depth) >> CLOSE)
            found.append(jnp.maximum(due, found[-1] + 1) if k else due)
        return found

    both_ends = [
        end_ticks(ends[0], jnp.where(final_block, 0, z)), end_ticks(ends[1], chips - 1 - z)
    ]
    my_ends = [jnp.where(c == 0, x, y) for x, y in zip(*both_ends)]
    grad_ticks = []
    for j, (x, y) in enumerate(zip(*both_ends)):
        due = jnp.maximum(jnp.maximum(x, y) + 1, state_base + own + j)
        grad_ticks.append(jnp.maximum(due, grad_ticks[-1] + 1) if j else due)
    ticks = grad_ticks[-1] + 1

    def listed(t, table):
        k, hit = jnp.int32(0), False
        for when in table:
            k += (when < t).astype(jnp.int32)
            hit = hit | (when == t)
        return hit, k

    def combine(k):
        h = 2 * k + c

        def part(slot):
            return pack[slot, h, 0], pack[slot, h, 1], pack[slot, h, 2]

        me, ae, re = part(c)
        mo, ao, ro = part(1 - c)
        mes = split(me)
        both_rows = mm(split(jnp.concatenate([mo, ro], 0)), mes, "nn")
        joined = both_rows[:D]
        back = both_rows[D:] + re
        aoe = mm(split(mo), split(ae), "nn") + ao
        both[k] = jnp.concatenate(
            [jnp.concatenate(split(joined), 1), jnp.concatenate(mes, 1)], 0
        )
        aup[k] = jnp.concatenate([aoe, ae], 0)
        whole = jnp.concatenate([back, joined], 0)
        duo[1, k] = whole

        @pl.when(leaf)
        def _():
            xout[k] = whole

    def tick(t, carry):
        q = third(t)
        step = t - STEPS * q
        in_group = t < heavy

        @pl.when(in_group & (step == 0))
        def _():
            group_start([q * QUAD + s for s in range(QUAD)], args, keep)

        @pl.when(in_group & (step == 1))
        def _():
            group_solve([q * QUAD + s for s in range(QUAD)], keep, spread)

        @pl.when(in_group & (step == 2))
        def _():
            group_end([q * QUAD + s for s in range(QUAD)], args, keep, pack, strengths)

            @pl.when(t == STEPS - 1)
            def _():
                begin()

            for s in range(2):
                pack_copy(2 * q + s).start()

        j = t - state_base

        @pl.when((j >= 0) & (j < own))
        def _():
            mid_copy(j).wait_recv()
            state_stage([2 * j, 2 * j + 1], args, keep, dq_ref)

        ok, kc = at(t, 0)

        @pl.when(ok)
        def _():
            pack_copy(kc).wait_recv()
            combine(kc)

            @pl.when(leaf & chained)
            def _():
                down_copy(kc).start()

        up_ok, ku = at(t, lag_up)
        down_ok, kd = at(t, lag_down)
        down_ok = down_ok & jnp.logical_not(leaf) & chained

        @pl.when(down_ok)
        def _():
            down_copy(kd).wait_recv()

        @pl.when(down_ok & jnp.logical_not(root & (o == 0)))
        def _():
            near = duo[1 - c, kd]
            back = mm(split(duo[c, kd]), split(near[D:]), "nn")
            xout[kd] = jnp.concatenate([back[:D] + near[:D], back[D:]], 0)

            @pl.when(jnp.logical_not(root))
            def _():
                down_copy(kd).start()

            @pl.when(root & jnp.logical_not(even))
            def _():
                pair_copy(kd).start()

        @pl.when(up_ok)
        def _():
            pltpu.make_async_copy(sin.at[ku], sin.at[ku], recv["state"].at[ku]).wait()
            state = sin[ku]
            moved = mm(pair_of(both, ku), split(state), "nn") + aup[ku]
            sout[ku] = moved[:D]
            mid = moved[D:]
            st[2 * ku + c] = jnp.where(c == 0, state, mid)
            sgive[ku] = jnp.where(c == 0, mid, state)

            @pl.when(jnp.logical_not(top))
            def _():
                up_copy(ku).start()

            mid_copy(ku).start()

        d_ok, k = listed(t, my_ends)

        @pl.when(d_ok & root & even)
        def _():
            pair_copy(k).wait_recv()

            @pl.when(o < n_outer - 2)
            def _():
                far_copy(k).wait_recv()

            end = pin[k, :D, :] + mm(split(dp[k]), split(pin[k, D:, :]), "nn")
            dz[k] = end

            @pl.when(o > 0)
            def _():
                eout[k] = xout[k, :D, :] + mm(split(end), split(xout[k, D:, :]), "nn")
                near_copy(k).start()
                far_copy(k).start()

        @pl.when(d_ok & landing)
        def _():
            relay_copy(k).wait_recv()

        @pl.when(d_ok & relays & (c == 0))
        def _():
            relay_copy(k).start()

        @pl.when(d_ok)
        def _():
            h = 2 * k + c
            end = dz[k]
            value = duo[c, k, :D, :] + mm(split(end), split(duo[c, k, D:, :]), "nn")

            @pl.when(relays & (c == 1))
            def _():
                vout[k] = value
                pass_copy(k).start()

            odd_end = jnp.where(c == 0, value, end)
            even_end = pack[1 - c, h, 2] + mm(split(odd_end), split(pack[1 - c, h, 0]), "nn")
            fin[h] = jnp.where(c == 0, even_end, odd_end)
            fgive[k] = jnp.where(c == 0, odd_end, even_end)
            fin_copy(k).start()

        hit, j = listed(t, grad_ticks)

        @pl.when(hit)
        def _():
            fin_copy(j).wait_recv()
            grad_stage([2 * j, 2 * j + 1], args, keep, dk_ref, dv_ref, accs)

        return carry

    lax.fori_loop(0, ticks, tick, 0)
    db, dg, xa, ya = (acc[...] for acc in accs)
    sums = jnp.concatenate([*split(xa), *split(ya)], 0)
    upper, lower = ones_where(row <= col), ones_where(row > col)
    dg = dg + dot(jnp.concatenate([upper, upper, lower, lower], 1), sums, "nn")
    db_ref[...] = db.T[:heads].astype(BF)
    dg_ref[...] = dg.T[:heads].astype(BF)

    for j in range(hpd):
        h = i * hpd + j
        owner = lax.rem(h, 2)

        @pl.when(i != owner)
        def _():
            pltpu.make_async_remote_copy(
                src_ref=s0_ref.at[j], dst_ref=sin.at[h // 2], send_sem=send["state"],
                recv_sem=recv["state"].at[h // 2], device_id=(o, owner), device_id_type=MESH,
            ).wait_send()

    def sent(kind, ref):
        every = ref.at[pl.ds(0, own)]
        pltpu.make_async_copy(every, every, send[kind]).wait()

    sent("pack", pack.at[0])
    sent("mid", sgive)
    sent("fin", fgive)

    @pl.when(jnp.logical_not(top))
    def _():
        sent("up", sout)

    @pl.when(jnp.logical_not(root) & chained)
    def _():
        sent("down", xout)

    @pl.when(root & jnp.logical_not(even))
    def _():
        sent("pair", xout)

    @pl.when(root & even & (o > 0))
    def _():
        sent("near", eout)
        sent("far", eout)

    @pl.when(relays)
    def _():
        sent("relay", dz)


def shards(n, n_outer, queries, key_rows, value_rows, beta_logit, log_gate, out_grad, block_states):
    heads = beta_logit.shape[1]
    own = heads // 2
    big = jax.ShapeDtypeStruct(queries.shape, BF)
    thin = jax.ShapeDtypeStruct((heads, C), BF)
    acc = pltpu.VMEM((C, D), F32)
    sems = pltpu.SemaphoreType.DMA((own,))
    dq, dk, dv, db, dg = pl.pallas_call(
        functools.partial(chain_kernel, heads, n, n_outer),
        out_shape=tuple(pltpu.VMEM(x.shape, x.dtype) for x in (big, big, big, thin, thin)),
        in_specs=[VM] * 7,
        out_specs=(VM,) * 5,
        scratch_shapes=[pltpu.VMEM((heads + 2, D, D), F32)] * len(KEPT)
        + [pltpu.VMEM((own + 1, D, D), F32)] * len(OWN)
        + [pltpu.VMEM((own + 1, 2 * D, D), F32)] * len(TWICE)
        + [
            pltpu.VMEM((2, heads, 3, D, D), F32),
            pltpu.VMEM((2, own + 1, 2 * D, D), F32),
            pltpu.VMEM((own + 1, 2 * D, 2 * D), BF),
            pltpu.VMEM((2 * C, (B - 1) * C), BF),
            pltpu.VMEM((heads, C), F32),
            acc, acc, acc, acc,
        ]
        + [pltpu.SemaphoreType.DMA] * len(SENDS) + [sems] * len(RECVS),
        compiler_params=pltpu.CompilerParams(
            vmem_limit_bytes=56 << 20, collective_id=0, has_side_effects=True
        ),
    )(beta_logit.T, log_gate.T, queries, key_rows, value_rows, out_grad, block_states[0])

    def hand_on(*refs):
        sem = refs[10]
        copies = [
            pltpu.make_async_copy(src, dst, sem.at[j])
            for j, (src, dst) in enumerate(zip(refs[:5], refs[5:10]))
        ]
        for copy in copies:
            copy.start()
        for copy in copies:
            copy.wait()

    dq, dk, dv, db, dg = pl.pallas_call(
        hand_on, out_shape=(big, big, big, thin, thin), in_specs=[VM] * 5,
        out_specs=(pl.BlockSpec(memory_space=pl.ANY),) * 5,
        scratch_shapes=[pltpu.SemaphoreType.DMA((5,))],
    )(*(pltpu.with_memory_space_constraint(x, pltpu.VMEM) for x in (dq, dk, dv, db, dg)))
    return dq, dk, dv, db.T, dg.T


def solution(mesh):
    wide = P(("outer", "inner"), None)
    return jax.shard_map(
        functools.partial(shards, mesh.shape["inner"], mesh.shape["outer"]),
        mesh=mesh,
        in_specs=(wide,) * 6 + (P("outer", "inner", None, None),),
        out_specs=(wide,) * 5,
        check_vma=False,
    )
```

```python
import functools

import jax
import jax.numpy as jnp
from jax import lax
from jax.experimental import pallas as pl
from jax.experimental.pallas import tpu as pltpu
from jax.sharding import PartitionSpec as P

D = 128
C = 128
B = 16
BF = jnp.bfloat16
F32 = jnp.float32
MESH = pl.DeviceIdType.MESH
VM = pl.BlockSpec(memory_space=pltpu.VMEM)
DIMS = {"nn": ((1,), (0,)), "nt": ((1,), (1,)), "tn": ((0,), (0,))}


def split(x):
    hi = x.astype(BF)
    return hi, (x - hi.astype(F32)).astype(BF)


def exact(x):
    return x.astype(BF), None


def dot(a, b, mode):
    return lax.dot_general(a, b, (DIMS[mode], ((), ())), preferred_element_type=F32)


def mm(a, b, mode):
    ka = 0 if mode == "tn" else 1
    kb = 1 if mode == "nt" else 0
    (ah, al), (bh, bl) = a, b
    if al is None and bl is None:
        return dot(ah, bh, mode)
    if al is None:
        return dot(jnp.concatenate([ah, ah], ka), jnp.concatenate([bh, bl], kb), mode)
    left = jnp.concatenate([ah, al], ka)
    if bl is None:
        return dot(left, jnp.concatenate([bh, bh], kb), mode)
    top = jnp.concatenate([bh, bl], 1 - kb)
    low = jnp.concatenate([bh, jnp.zeros_like(bl)], 1 - kb)
    both = dot(left, jnp.concatenate([top, low], kb), mode)
    n = both.shape[1] // 2
    return both[:, :n] + both[:, n:]


def iotas():
    return lax.broadcasted_iota(jnp.int32, (C, C), 0), lax.broadcasted_iota(jnp.int32, (C, C), 1)


def ones_where(mask):
    return jnp.where(mask, 1.0, 0.0).astype(BF)


def unit(x):
    r = lax.rsqrt(jnp.sum(x * x, axis=1, keepdims=True) + 1e-06)
    return x * r, r


def decays(gate, row, col):
    wide = gate
    rhs = jnp.concatenate([wide, jnp.where(row > col, wide, 0.0)], 1).astype(BF)
    both = dot(ones_where(row >= col), rhs, "nn")
    after = dot(ones_where(row < col), wide.astype(BF), "nn")
    pair = jnp.where(row >= col, jnp.exp(both[:, C:]), 0.0)
    return jnp.exp(both[:, :C]), jnp.exp(after), pair


def same_block(row, col, size):
    return row // size == col // size


def inverses(lowers, row, col, spread):
    r, lane = row[:B], col[:B]
    packed = []
    for low in lowers:
        parts = [
            jnp.where(lane // B == g, low[g * B : (g + 1) * B], 0.0) for g in range(C // B)
        ]
        while len(parts) > 1:
            parts = [a + b for a, b in zip(parts[::2], parts[1::2])]
        packed.append(parts[0])
    factors = dot(jnp.concatenate(split(jnp.concatenate(packed, 0)), 1), spread[...], "nn")
    small = [jnp.where(lane % B == r, 1.0, 0.0) for _ in lowers]
    for j in range(B - 1):
        small = [
            x - factors[h * B : (h + 1) * B, j * C : (j + 1) * C] * x[j : j + 1]
            for h, x in enumerate(small)
        ]
    done = [
        jnp.concatenate([jnp.where(lane // B == g, x, 0.0) for g in range(C // B)], 0)
        for x in small
    ]
    size = B
    while size < C:
        pick = same_block(row, col, 2 * size) & (row // size != col // size)
        halves = [split(t) for t in done]
        mids = [mm(t, split(jnp.where(pick, low, 0.0)), "nn") for t, low in zip(halves, lowers)]
        done = [t - mm(split(m), h, "nn") for t, m, h in zip(done, mids, halves)]
        size *= 2
    return done


def head_columns(b_ref, g_ref, h):
    heads = b_ref.shape[0]
    pick = ones_where(lax.broadcasted_iota(jnp.int32, (heads, C), 0) == h)
    return jax.nn.sigmoid(dot(b_ref[...], pick, "tn")), dot(g_ref[...], pick, "tn")


def grams(q, k, qr, kr, pair, row, col):
    across = jnp.sum(jnp.where(row == col, kr, 0.0), axis=0, keepdims=True)
    both = dot(jnp.concatenate([q, k], 0), k, "nt")
    scaled = pair * across
    return both[:C] * (qr * scaled), jnp.where(row > col, both[C:] * (kr * scaled), 0.0)


def columns(h):
    return pl.ds(pl.multiple_of(h * D, D), D)


def group_start(hs, args, keep):
    b_ref, g_ref, q_ref, k_ref, _, c_ref = args
    row, col = iotas()
    cols = [head_columns(b_ref, g_ref, h) for h in hs]
    qus = [unit(q_ref[:, columns(h)].astype(F32)) for h in hs]
    qns = [qu[0] for qu in qus]
    krs = [unit(k_ref[:, columns(h)].astype(F32))[1] for h in hs]
    decs = [decays(gate, row, col) for _, gate in cols]
    gms = [
        grams(q_ref[:, columns(h)], k_ref[:, columns(h)], qu[1], kr, d[2], row, col)
        for h, qu, kr, d in zip(hs, qus, krs, decs)
    ]
    cots = [exact(c_ref[:, columns(h)]) for h in hs]
    qparts = [mm(cot, split(qn * d[0]), "tn") for cot, qn, d in zip(cots, qns, decs)]
    pcs = [mm(split(scores), cot, "tn") for (scores, _), cot in zip(gms, cots)]
    for j, h in enumerate(hs):
        for name, value in (
            ("beta", cols[j][0]), ("growth", decs[j][0]), ("tail", decs[j][1]),
            ("pair", decs[j][2]), ("scores", gms[j][0]), ("gram", gms[j][1]),
            ("pc", pcs[j]), ("x", qparts[j]),
        ):
            keep[name][h] = value


def group_solve(hs, keep, spread):
    row, col = iotas()
    lowers = [keep["beta"][h] * keep["gram"][h] for h in hs]
    for h, inv in zip(hs, inverses(lowers, row, col, spread)):
        keep["inv"][h] = inv


def group_end(hs, args, keep, pack, strengths):
    _, _, _, k_ref, v_ref, _ = args
    row, col = iotas()
    eye = row == col
    kns = [unit(k_ref[:, columns(h)].astype(F32))[0] for h in hs]
    grows = [keep["growth"][h] for h in hs]
    invs = [split(keep["inv"][h] * strengths[pl.ds(h, 1), :]) for h in hs]
    wks = [mm(i, split(g * kn), "nn") for i, g, kn in zip(invs, grows, kns)]
    wvs = [mm(i, exact(v_ref[:, columns(h)]), "nn") for i, h in zip(invs, hs)]
    tks = [kn * keep["tail"][h] for kn, h in zip(kns, hs)]
    wss = [split(wk) for wk in wks]
    lasts = [jnp.where(eye, jnp.broadcast_to(g[C - 1 :, :], (C, C)), 0.0) for g in grows]
    lefts = [split(jnp.concatenate([tk, keep["pc"][h]], 1)) for h, tk in zip(hs, tks)]
    outs = [mm(left, ws, "tn") for left, ws in zip(lefts, wss)]
    ms = [last - out[:D] for last, out in zip(lasts, outs)]
    rs = [keep["x"][h] - out[D:] for h, out in zip(hs, outs)]
    ads = [mm((left[0][:, :D], left[1][:, :D]), split(wv), "tn") for left, wv in zip(lefts, wvs)]
    for j, h in enumerate(hs):
        keep["wk"][h] = wks[j]
        keep["wv"][h] = wvs[j]
        pack[0, h, 0] = ms[j]
        pack[0, h, 1] = ads[j]
        pack[0, h, 2] = rs[j]


def state_stage(hs, args, keep, dq_ref):
    _, _, q_ref, k_ref, _, c_ref = args
    qus = [unit(q_ref[:, columns(h)].astype(F32)) for h in hs]
    kns = [unit(k_ref[:, columns(h)].astype(F32))[0] for h in hs]
    cots = [exact(c_ref[:, columns(h)]) for h in hs]
    sss = [split(keep["st"][h]) for h in hs]
    news = [keep["wv"][h] - mm(split(keep["wk"][h]), ss, "nn") for h, ss in zip(hs, sss)]
    dqgs = [keep["growth"][h] * mm(cot, ss, "nt") for h, cot, ss in zip(hs, cots, sss)]
    dscs = [mm(cot, split(new), "nt") for cot, new in zip(cots, news)]
    b1s = [split(dsc * keep["pair"][h]) for h, dsc in zip(hs, dscs)]
    dqns = [mm(b1, split(kn), "nn") + dqg for b1, kn, dqg in zip(b1s, kns, dqgs)]
    wks = [mm(b1, split(qn), "tn") for b1, (qn, _) in zip(b1s, qus)]
    dqs = [
        (qr * (dqn - qn * jnp.sum(dqn * qn, axis=1, keepdims=True))).astype(BF)
        for (qn, qr), dqn in zip(qus, dqns)
    ]
    zs = [dsc * keep["scores"][h] for h, dsc in zip(hs, dscs)]
    for j, h in enumerate(hs):
        dq_ref[:, columns(h)] = dqs[j]
        keep["wv"][h] = news[j]
        keep["wk"][h] = wks[j]
        keep["z"][h] = zs[j]
        keep["x"][h] = dqgs[j] * qus[j][0]


def grad_stage(hs, args, keep, dk_ref, dv_ref, accs):
    _, _, _, k_ref, v_ref, _ = args
    row, col = iotas()
    upper = ones_where(row <= col)
    upper2 = jnp.concatenate([upper, upper], 1)
    lane = lax.broadcasted_iota(jnp.int32, accs[0].shape, 1)
    at = range(len(hs))
    kus = [unit(k_ref[:, columns(h)].astype(F32)) for h in hs]
    betas, grows, tails = ([keep[x][h] for h in hs] for x in ("beta", "growth", "tail"))
    fss = [split(keep["fin"][h]) for h in hs]
    tks = [ku[0] * tail for ku, tail in zip(kus, tails)]
    dnews = [keep["pc"][h] + mm(split(tk), fs, "nt") for h, tk, fs in zip(hs, tks, fss)]
    nss = [split(keep["wv"][h]) for h in hs]
    errs = [mm(split(keep["inv"][h]), split(dnew), "tn") for h, dnew in zip(hs, dnews)]
    dtks = [mm(ns, fs, "nn") for ns, fs in zip(nss, fss)]
    ess = [split(err) for err in errs]
    dlows = [jnp.where(row > col, -mm(es, ns, "nt"), 0.0) for es, ns in zip(ess, nss)]
    dkws = [-mm(es, split(keep["st"][h]), "nt") for es, h in zip(ess, hs)]
    b2s = [dlows[j] * betas[j] * keep["pair"][h] for j, h in enumerate(hs)]
    kss = [split(ku[0]) for ku in kus]
    kgs = [g * d for g, d in zip(grows, dkws)]
    dkns = [
        keep["wk"][h] + mm(split(b2s[j] + b2s[j].T), kss[j], "nn")
        + betas[j] * kgs[j] + tails[j] * dtks[j]
        for j, h in enumerate(hs)
    ]
    dlgs = [dlows[j] * keep["gram"][h] for j, h in enumerate(hs)]
    kgs = [ku[0] * kg for ku, kg in zip(kus, kgs)]
    ups = [
        dot(upper2, jnp.concatenate(split(keep["z"][h] + betas[j] * dlgs[j]), 0), "nn")
        for j, h in enumerate(hs)
    ]
    xs = [
        jnp.sum(keep["x"][h] + betas[j] * kgs[j], axis=1, keepdims=True) for j, h in enumerate(hs)
    ]
    ys = [jnp.sum(dtk * tk, axis=1, keepdims=True) for dtk, tk in zip(dtks, tks)]
    dks = [
        (kr * (dkn - kn * jnp.sum(dkn * kn, axis=1, keepdims=True))).astype(BF)
        for (kn, kr), dkn in zip(kus, dkns)
    ]
    dbetas = [
        jnp.sum(
            (dlgs[j] + kgs[j] + errs[j] * v_ref[:, columns(h)].astype(F32))
            * (betas[j] * (1.0 - betas[j])), axis=1, keepdims=True,
        )
        for j, h in enumerate(hs)
    ]
    totals = [
        jnp.sum(
            jnp.sum(keep["st"][h] * keep["fin"][h].T * grows[j][C - 1 :, :], axis=1, keepdims=True),
            axis=0, keepdims=True,
        )
        for j, h in enumerate(hs)
    ]
    dgates = [
        totals[j] + jnp.sum(
            jnp.where(row > col, ups[j], 0.0), axis=1, keepdims=True,
        )
        for j in at
    ]
    db, dg, xa, ya = (a[...] for a in accs)
    for j, h in enumerate(hs):
        dk_ref[:, columns(h)] = dks[j]
        dv_ref[:, columns(h)] = (betas[j] * errs[j]).astype(BF)
        db, dg = jnp.where(lane == h, dbetas[j], db), jnp.where(lane == h, dgates[j], dg)
        xa, ya = jnp.where(lane == h, xs[j], xa), jnp.where(lane == h, ys[j], ya)
    for acc, value in zip(accs, (db, dg, xa, ya)):
        acc[...] = value


KEPT = (
    "inv", "wk", "wv", "pc", "beta", "growth", "tail",
    "pair", "scores", "gram", "z", "x", "st", "fin",
)
OWN = ("sin", "sout", "sgive", "dz", "dp", "eout", "fgive", "vout")
TWICE = ("aup", "xout", "pin")
SENDS = ("state", "pack", "up", "mid", "down", "pair", "near", "far", "relay", "fin")
RECVS = ("state", "pack", "mid", "down", "pair", "far", "relay", "fin")
QUAD, DUO = 4, 2
STEPS = 3
HOP_UP, HOP, HOP_OUT, HOP_BACK = 3, 3, 2, 4
LATE_UP = 2
CLOSE = 2


def pair_of(ref, k):
    return ref[k, :, :D], ref[k, :, D:]


def chain_kernel(
    heads, n, n_outer,
    b_ref, g_ref, q_ref, k_ref, v_ref, c_ref, s0_ref,
    dq_ref, dk_ref, dv_ref, db_ref, dg_ref,
    *scratch,
):
    args = (b_ref, g_ref, q_ref, k_ref, v_ref, c_ref)
    scratch = list(scratch)
    keep = {x: scratch.pop(0) for x in KEPT}
    sin, sout, sgive, dz, dp, eout, fgive, vout = (scratch.pop(0) for _ in OWN)
    aup, xout, pin = (scratch.pop(0) for _ in TWICE)
    pack, duo, both, spread, strengths = (scratch.pop(0) for _ in range(5))
    accs = [scratch.pop(0) for _ in range(4)]
    send = {x: scratch.pop(0) for x in SENDS}
    recv = {x: scratch.pop(0) for x in RECVS}
    st, fin = keep["st"], keep["fin"]
    o, i = lax.axis_index("outer"), lax.axis_index("inner")
    z, c = i // 2, lax.rem(i, 2)
    chips, own, quads = n // 2, heads // 2, heads // QUAD
    hpd = s0_ref.shape[0]
    top = z == chips - 1
    zz = jnp.where(c == 0, z, chips - 1 - z)
    root, leaf = zz == 0, zz == chips - 1
    final_block = o == n_outer - 1
    even = lax.rem(o, 2) == 0
    barrier = pltpu.get_barrier_semaphore()
    for d in range(1, n):
        pl.semaphore_signal(
            barrier, inc=1, device_id=(o, lax.rem(i + d, n)), device_id_type=MESH
        )
    for d in range(1, n_outer):
        pl.semaphore_signal(
            barrier, inc=1, device_id=(lax.rem(o + d, n_outer), i), device_id_type=MESH
        )

    def remote(src, dst, give, take, k, target):
        return pltpu.make_async_remote_copy(
            src_ref=src, dst_ref=dst, send_sem=send[give], recv_sem=recv[take].at[k],
            device_id=target, device_id_type=MESH,
        )

    mate = (o, i + 1 - 2 * c)
    above = (o, lax.rem(i + 2, n))
    inward = (o, lax.rem(i + n - 2 + 4 * c, n))
    outward = (o, lax.rem(i + n + 2 - 4 * c, n))
    before = (lax.rem(o + n_outer - 1, n_outer), i)
    before2 = (lax.rem(o + n_outer - 2, n_outer), i)

    def pack_copy(k):
        h = 2 * k + 1 - c
        return remote(pack.at[0, h], pack.at[1, h], "pack", "pack", k, mate)

    def up_copy(k):
        return remote(sout.at[k], sin.at[k], "up", "state", k, above)

    def mid_copy(k):
        return remote(sgive.at[k], st.at[2 * k + c], "mid", "mid", k, mate)

    def down_copy(k):
        return remote(xout.at[k], duo.at[0, k], "down", "down", k, inward)

    def pair_copy(k):
        return remote(xout.at[k], pin.at[k], "pair", "pair", k, before)

    def near_copy(k):
        return remote(eout.at[k], dz.at[k], "near", "relay", k, before)

    def far_copy(k):
        return remote(eout.at[k], dp.at[k], "far", "far", k, before2)

    def relay_copy(k):
        return remote(dz.at[k], dz.at[k], "relay", "relay", k, outward)

    def pass_copy(k):
        return remote(vout.at[k], dz.at[k], "relay", "relay", k, outward)

    def fin_copy(k):
        return remote(fgive.at[k], fin.at[2 * k + c], "fin", "fin", k, mate)

    for j in range(hpd):
        h = i * hpd + j

        @pl.when(i == lax.rem(h, 2))
        def _():
            k = h // 2
            pltpu.make_async_copy(s0_ref.at[j], sin.at[k], recv["state"].at[k]).start()

    def begin():
        pl.semaphore_wait(barrier, n + n_outer - 2)
        for j in range(hpd):
            h = i * hpd + j
            owner = lax.rem(h, 2)

            @pl.when(i != owner)
            def _():
                pltpu.make_async_remote_copy(
                    src_ref=s0_ref.at[j], dst_ref=sin.at[h // 2], send_sem=send["state"],
                    recv_sem=recv["state"].at[h // 2], device_id=(o, owner), device_id_type=MESH,
                ).start()

    row, col = iotas()
    for j in range(B - 1):
        ones = ones_where(same_block(row, col, B) & (row % B == j))
        spread[:, j * C : (j + 1) * C] = jnp.concatenate([ones, ones], 0)
    strengths[...] = jax.nn.sigmoid(b_ref[...].astype(F32))
    for acc in accs:
        acc[...] = jnp.zeros_like(acc)

    @pl.when(final_block & ((c == 0) | root))
    def _():
        dz[...] = jnp.zeros_like(dz)

    @pl.when((o == n_outer - 2) & root)
    def _():
        dp[...] = jnp.zeros_like(dp)

    @pl.when(leaf)
    def _():
        row, col = iotas()
        ident = jnp.where(row == col, 1.0, 0.0)
        for k in range(own):
            duo[0, k] = jnp.concatenate([jnp.zeros_like(ident), ident], 0)

    relays = jnp.logical_not(leaf) & (jnp.logical_not(final_block) | (c == 1))
    landing = jnp.where(root, jnp.logical_not(even | final_block), jnp.logical_not(final_block) | (c == 1))
    lag_down = HOP * (chips - 1 - zz)
    lag_root = HOP * (chips - 1) + HOP_OUT * (n_outer // 2 - o // 2)
    ends = [
        jnp.where(final_block, HOP * (chips - 1 - z), lag_root + HOP_BACK * z),
        jnp.where(final_block, 0, lag_root) + HOP_BACK * (chips - 1 - z),
    ]
    lag_up = LATE_UP + HOP_UP * z

    def third(x):
        return (x * 43) >> 7

    def start_of(k):
        return STEPS * (k >> 1) + (k & 1) + STEPS

    def at(t, lag):
        late = t - lag - STEPS
        whole = third(late)
        part = late - STEPS * whole
        k = 2 * whole + part
        ok = (late >= 0) & (part < 2) & (k < own)
        return ok, k

    heavy = STEPS * quads
    last_start = STEPS * ((own - 1) // 2) + (own - 1) % 2 + STEPS
    state_base = jnp.maximum(heavy, last_start + lag_up + 1 - (own - 1))
    def end_ticks(lag, depth):
        found = []
        for k in range(own):
            due = start_of(k) + lag - ((k * depth) >> CLOSE)
            found.append(jnp.maximum(due, found[-1] + 1) if k else due)
        return found

    both_ends = [
        end_ticks(ends[0], jnp.where(final_block, 0, z)), end_ticks(ends[1], chips - 1 - z)
    ]
    my_ends = [jnp.where(c == 0, x, y) for x, y in zip(*both_ends)]
    grad_ticks = []
    for j, (x, y) in enumerate(zip(*both_ends)):
        due = jnp.maximum(jnp.maximum(x, y) + 1, state_base + own + j)
        grad_ticks.append(jnp.maximum(due, grad_ticks[-1] + 1) if j else due)
    ticks = grad_ticks[-1] + 1

    def listed(t, table):
        k, hit = jnp.int32(0), False
        for when in table:
            k += (when < t).astype(jnp.int32)
            hit = hit | (when == t)
        return hit, k

    def combine(k):
        h = 2 * k + c

        def part(slot):
            return pack[slot, h, 0], pack[slot, h, 1], pack[slot, h, 2]

        me, ae, re = part(c)
        mo, ao, ro = part(1 - c)
        mes = split(me)
        both_rows = mm(split(jnp.concatenate([mo, ro], 0)), mes, "nn")
        joined = both_rows[:D]
        back = both_rows[D:] + re
        aoe = mm(split(mo), split(ae), "nn") + ao
        both[k] = jnp.concatenate(
            [jnp.concatenate(split(joined), 1), jnp.concatenate(mes, 1)], 0
        )
        aup[k] = jnp.concatenate([aoe, ae], 0)
        whole = jnp.concatenate([back, joined], 0)
        duo[1, k] = whole

        @pl.when(leaf)
        def _():
            xout[k] = whole

    def tick(t, carry):
        q = third(t)
        step = t - STEPS * q
        in_group = t < heavy

        @pl.when(in_group & (step == 0))
        def _():
            group_start([q * QUAD + s for s in range(QUAD)], args, keep)

        @pl.when(in_group & (step == 1))
        def _():
            group_solve([q * QUAD + s for s in range(QUAD)], keep, spread)

        @pl.when(in_group & (step == 2))
        def _():
            group_end([q * QUAD + s for s in range(QUAD)], args, keep, pack, strengths)

            @pl.when(t == STEPS - 1)
            def _():
                begin()

            for s in range(2):
                pack_copy(2 * q + s).start()

        j = t - state_base

        @pl.when((j >= 0) & (j < own))
        def _():
            mid_copy(j).wait_recv()
            state_stage([2 * j, 2 * j + 1], args, keep, dq_ref)

        ok, kc = at(t, 0)

        @pl.when(ok)
        def _():
            pack_copy(kc).wait_recv()
            combine(kc)

            @pl.when(leaf)
            def _():
                down_copy(kc).start()

        up_ok, ku = at(t, lag_up)
        down_ok, kd = at(t, lag_down)
        down_ok = down_ok & jnp.logical_not(leaf)

        @pl.when(down_ok)
        def _():
            down_copy(kd).wait_recv()
            near = duo[1 - c, kd]
            back = mm(split(duo[c, kd]), split(near[D:]), "nn")
            xout[kd] = jnp.concatenate([back[:D] + near[:D], back[D:]], 0)

            @pl.when(jnp.logical_not(root))
            def _():
                down_copy(kd).start()

            @pl.when(root & jnp.logical_not(even))
            def _():
                pair_copy(kd).start()

        @pl.when(up_ok)
        def _():
            pltpu.make_async_copy(sin.at[ku], sin.at[ku], recv["state"].at[ku]).wait()
            state = sin[ku]
            moved = mm(pair_of(both, ku), split(state), "nn") + aup[ku]
            sout[ku] = moved[:D]
            mid = moved[D:]
            st[2 * ku + c] = jnp.where(c == 0, state, mid)
            sgive[ku] = jnp.where(c == 0, mid, state)

            @pl.when(jnp.logical_not(top))
            def _():
                up_copy(ku).start()

            mid_copy(ku).start()

        d_ok, k = listed(t, my_ends)

        @pl.when(d_ok & root & even)
        def _():
            pair_copy(k).wait_recv()

            @pl.when(o < n_outer - 2)
            def _():
                far_copy(k).wait_recv()

            end = pin[k, :D, :] + mm(split(dp[k]), split(pin[k, D:, :]), "nn")
            dz[k] = end

            @pl.when(o > 0)
            def _():
                eout[k] = xout[k, :D, :] + mm(split(end), split(xout[k, D:, :]), "nn")
                near_copy(k).start()
                far_copy(k).start()

        @pl.when(d_ok & landing)
        def _():
            relay_copy(k).wait_recv()

        @pl.when(d_ok & relays & (c == 0))
        def _():
            relay_copy(k).start()

        @pl.when(d_ok)
        def _():
            h = 2 * k + c
            end = dz[k]
            value = duo[c, k, :D, :] + mm(split(end), split(duo[c, k, D:, :]), "nn")

            @pl.when(relays & (c == 1))
            def _():
                vout[k] = value
                pass_copy(k).start()

            odd_end = jnp.where(c == 0, value, end)
            even_end = pack[1 - c, h, 2] + mm(split(odd_end), split(pack[1 - c, h, 0]), "nn")
            fin[h] = jnp.where(c == 0, even_end, odd_end)
            fgive[k] = jnp.where(c == 0, odd_end, even_end)
            fin_copy(k).start()

        hit, j = listed(t, grad_ticks)

        @pl.when(hit)
        def _():
            fin_copy(j).wait_recv()
            grad_stage([2 * j, 2 * j + 1], args, keep, dk_ref, dv_ref, accs)

        return carry

    lax.fori_loop(0, ticks, tick, 0)
    db, dg, xa, ya = (acc[...] for acc in accs)
    sums = jnp.concatenate([*split(xa), *split(ya)], 0)
    upper, lower = ones_where(row <= col), ones_where(row > col)
    dg = dg + dot(jnp.concatenate([upper, upper, lower, lower], 1), sums, "nn")
    db_ref[...] = db.T[:heads].astype(BF)
    dg_ref[...] = dg.T[:heads].astype(BF)

    for j in range(hpd):
        h = i * hpd + j
        owner = lax.rem(h, 2)

        @pl.when(i != owner)
        def _():
            pltpu.make_async_remote_copy(
                src_ref=s0_ref.at[j], dst_ref=sin.at[h // 2], send_sem=send["state"],
                recv_sem=recv["state"].at[h // 2], device_id=(o, owner), device_id_type=MESH,
            ).wait_send()

    def sent(kind, ref):
        every = ref.at[pl.ds(0, own)]
        pltpu.make_async_copy(every, every, send[kind]).wait()

    sent("pack", pack.at[0])
    sent("mid", sgive)
    sent("fin", fgive)

    @pl.when(jnp.logical_not(top))
    def _():
        sent("up", sout)

    @pl.when(jnp.logical_not(root))
    def _():
        sent("down", xout)

    @pl.when(root & jnp.logical_not(even))
    def _():
        sent("pair", xout)

    @pl.when(root & even & (o > 0))
    def _():
        sent("near", eout)
        sent("far", eout)

    @pl.when(relays)
    def _():
        sent("relay", dz)


def shards(n, n_outer, queries, key_rows, value_rows, beta_logit, log_gate, out_grad, block_states):
    heads = beta_logit.shape[1]
    own = heads // 2
    big = jax.ShapeDtypeStruct(queries.shape, BF)
    thin = jax.ShapeDtypeStruct((heads, C), BF)
    acc = pltpu.VMEM((C, D), F32)
    sems = pltpu.SemaphoreType.DMA((own,))
    dq, dk, dv, db, dg = pl.pallas_call(
        functools.partial(chain_kernel, heads, n, n_outer),
        out_shape=tuple(pltpu.VMEM(x.shape, x.dtype) for x in (big, big, big, thin, thin)),
        in_specs=[VM] * 7,
        out_specs=(VM,) * 5,
        scratch_shapes=[pltpu.VMEM((heads + 2, D, D), F32)] * len(KEPT)
        + [pltpu.VMEM((own + 1, D, D), F32)] * len(OWN)
        + [pltpu.VMEM((own + 1, 2 * D, D), F32)] * len(TWICE)
        + [
            pltpu.VMEM((2, heads, 3, D, D), F32),
            pltpu.VMEM((2, own + 1, 2 * D, D), F32),
            pltpu.VMEM((own + 1, 2 * D, 2 * D), BF),
            pltpu.VMEM((2 * C, (B - 1) * C), BF),
            pltpu.VMEM((heads, C), F32),
            acc, acc, acc, acc,
        ]
        + [pltpu.SemaphoreType.DMA] * len(SENDS) + [sems] * len(RECVS),
        compiler_params=pltpu.CompilerParams(
            vmem_limit_bytes=56 << 20, collective_id=0, has_side_effects=True
        ),
    )(beta_logit.T, log_gate.T, queries, key_rows, value_rows, out_grad, block_states[0])

    def hand_on(*refs):
        sem = refs[10]
        copies = [
            pltpu.make_async_copy(src, dst, sem.at[j])
            for j, (src, dst) in enumerate(zip(refs[:5], refs[5:10]))
        ]
        for copy in copies:
            copy.start()
        for copy in copies:
            copy.wait()

    dq, dk, dv, db, dg = pl.pallas_call(
        hand_on, out_shape=(big, big, big, thin, thin), in_specs=[VM] * 5,
        out_specs=(pl.BlockSpec(memory_space=pl.ANY),) * 5,
        scratch_shapes=[pltpu.SemaphoreType.DMA((5,))],
    )(*(pltpu.with_memory_space_constraint(x, pltpu.VMEM) for x in (dq, dk, dv, db, dg)))
    return dq, dk, dv, db.T, dg.T


def solution(mesh):
    wide = P(("outer", "inner"), None)
    return jax.shard_map(
        functools.partial(shards, mesh.shape["inner"], mesh.shape["outer"]),
        mesh=mesh,
        in_specs=(wide,) * 6 + (P("outer", "inner", None, None),),
        out_specs=(wide,) * 5,
        check_vma=False,
    )
```
